128 devices in a mesh: freq: 8 (over x, core), blk: 16 (over y, z).
Axes of the slice: x: 4, y: 4, z: 4, core: 2. Of those that a mesh axis runs over, the one named last changes fastest.
Arguments:
- sky_maps: bfloat16 [8, 256, 32, 8192], P('freq', 'blk'), may hold values from -24 to 24
- legendre: bfloat16 [128, 256, 4096], P('blk')
- mode_values: int32 [128], replicated, may hold values from 0 to 4095, as said below
- cycle_order: int32 [256], replicated, may hold values from 0 to 255, each once
- bin_widths: int32 [128], replicated, may hold values from 1 to 512, 4096 in all
Outputs:
- cleaned: float32 [32, 2, 128, 4096], P(None, None, None, ('freq', 'blk'))
The draws below stay inside these ranges and needn't reach their ends.
Inputs may be any that keep to these rules, and one draw needn't show every extreme that they name: Distinct values, 0 and 4095 among them; legendre[s, q, l] is zero wherever l < mode_values[s]. `cycle_order`: each cycle index once.
All inputs are finite; a program needn't handle non-finite values.
Results may differ from the reference program's by a relative error of at most 0.0036.
Values may be sent and summed in bfloat16 or wider, within the bound.
A program may use at most 192 MiB of HBM per device.

```python
import math
import jax
import jax.numpy as jnp
import numpy as np
from jax import lax

NPHI = 8192
L = 4096
NBINS = 128
KMAPS = 32
M_DEV = 8
NCHAN = 8
CYCLES = 256
M = 128


def pick_modes(key):
    inner = jax.random.permutation(jax.random.fold_in(key, 11), L - 2)[:M - 2].astype(jnp.int32) + 1
    values_sorted = jnp.sort(jnp.concatenate([jnp.array([0, L - 1], jnp.int32), inner]))
    slot_table = jnp.arange(M, dtype=jnp.int32).reshape(M_DEV, M // M_DEV)
    odd_rows = jnp.arange(M_DEV, dtype=jnp.int32)[:, None] % 2 == 1
    flipped = jnp.where(odd_rows, slot_table[:, ::-1], slot_table)
    return values_sorted[flipped.T.reshape(M)]


def draw_mode_values(key, part):
    return pick_modes(key)


def draw_legendre(key, part):
    modes_drawn = pick_modes(key)
    first_key, second_key = jax.random.split(jax.random.fold_in(key, 23))
    values_base = jnp.clip(jax.random.normal(first_key, (M, CYCLES, L), jnp.float32), -6.0, 6.0)
    factor = jnp.exp(jax.random.uniform(second_key, (M, CYCLES, 1), jnp.float32, math.log(0.3), math.log(3.0)))
    ell_values = jnp.arange(L, dtype=jnp.int32)
    live_mask = (ell_values[None, None, :] >= modes_drawn[:, None, None]).astype(jnp.float32)
    return (values_base * factor * live_mask * jnp.float32(CYCLES ** (-0.5))).astype(jnp.bfloat16)


def draw_sky_maps(key, part):
    first_key, second_key, third_key = jax.random.split(jax.random.fold_in(key, 37), 3)
    common = jax.random.normal(first_key, (1, CYCLES, KMAPS, NPHI), jnp.float32)
    noise = jax.random.normal(second_key, (NCHAN, CYCLES, KMAPS, NPHI), jnp.float32)
    factor = jnp.exp(jax.random.uniform(third_key, (NCHAN, CYCLES, 1, 1), jnp.float32, math.log(0.3), math.log(3.0)))
    return jnp.clip(common + noise * factor, -24.0, 24.0).astype(jnp.bfloat16)


def length_profile(count, total, bound, slope):
    weights = [(1 << 20) // math.isqrt(standing ** slope) + 1 for standing in range(2, count + 1)]
    surplus, given = total - bound - (count - 1), [1] * (count - 1)
    while surplus > 0:
        free = [i for i in range(count - 1) if given[i] < bound]
        whole, left = sum([weights[i] for i in free]), surplus
        for i in free:
            more = min(bound - given[i], max(1, left * weights[i] // whole), surplus)
            given[i] = given[i] + more
            surplus = surplus - more
    return np.array([bound] + given)


def ragged(rng, number_of, total, reach, skew):
    if number_of == 2:
        one = jax.random.randint(rng, (), max(1, total - reach), min(reach, total - 1) + 1)
        return jnp.stack([one, total - one])
    tallies = jnp.asarray(length_profile(number_of, total, reach, skew), jnp.int32)
    twos = (number_of - 1) // 2
    donor, taker = tallies[1:1 + 2 * twos:2], tallies[2:2 + 2 * twos:2]
    slack = jnp.minimum(donor - 1, reach - taker)
    passed = jax.random.randint(jax.random.fold_in(rng, 1), (twos,), 0, 1 << 20) % (slack + 1)
    tallies = tallies.at[1:1 + 2 * twos:2].set(donor - passed).at[2:2 + 2 * twos:2].set(taker + passed)
    return tallies[jax.random.permutation(jax.random.fold_in(rng, 2), number_of)]


def setup_inputs(seed: int = 0) -> dict:
    keys = jax.random.split(jax.random.key(seed), 6)
    sky_maps = draw_sky_maps(jax.random.fold_in(keys[5], 71), 0)
    legendre = draw_legendre(jax.random.fold_in(keys[5], 71), 0)
    mode_values = draw_mode_values(jax.random.fold_in(keys[5], 71), 0)
    cycle_order = jax.random.permutation(keys[3], CYCLES).astype(jnp.int32)
    bin_widths = ragged(keys[4], NBINS, L, L // 8, 0).astype(jnp.int32)
    return {"sky_maps": sky_maps, "legendre": legendre, "mode_values": mode_values, "cycle_order": cycle_order, "bin_widths": bin_widths}


def build_trig(mode_values, pixel_count):
    pixels = jnp.arange(pixel_count, dtype=jnp.int32)
    phase_index = pixels[:, None] * mode_values[None, :].astype(jnp.int32) % pixel_count
    angles = phase_index.astype(jnp.float32) * jnp.float32(2.0 * math.pi / pixel_count)
    factor = jnp.float32(pixel_count ** (-0.5))
    return (jnp.cos(angles) * factor, -jnp.sin(angles) * factor)

def ilc_weights(spectra):
    chan_count = spectra.shape[1]
    trace_value = jnp.trace(spectra, axis1=1, axis2=2)
    identity = jnp.eye(chan_count, dtype=jnp.float32)
    loaded = spectra + (jnp.float32(0.1) * trace_value / jnp.float32(chan_count))[:, None, None] * identity[None]
    lower_factor = jnp.linalg.cholesky(loaded)
    unit_vector = jnp.ones(spectra.shape[:2] + (1,), jnp.float32)
    forward = jax.scipy.linalg.solve_triangular(lower_factor, unit_vector, lower=True)
    solved = jax.scipy.linalg.solve_triangular(lower_factor, forward, trans=1, lower=True)[..., 0]
    return solved / jnp.sum(solved, axis=1, keepdims=True)

def reference(sky_maps, legendre, mode_values, cycle_order, bin_widths):
    cos_part, sin_part = build_trig(mode_values, NPHI)
    fourier = jnp.concatenate([cos_part, sin_part], axis=1).astype(jnp.bfloat16)
    inverse = jnp.argsort(cycle_order).astype(jnp.int32)

    def one_channel(channel_map):
        flat = channel_map.reshape(CYCLES * KMAPS, NPHI)
        rows_out = jnp.dot(flat.astype(jnp.float32), fourier.astype(jnp.float32), preferred_element_type=jnp.float32).astype(jnp.bfloat16)
        return rows_out.reshape(CYCLES, KMAPS, 2 * M)[inverse]
    ordered = lax.map(one_channel, sky_maps)
    per_mode = ordered.reshape(NCHAN, CYCLES, KMAPS, 2, M).transpose(4, 1, 0, 2, 3).reshape(M, CYCLES, NCHAN * KMAPS * 2)

    def one_mode(pair):
        left_side, table_rows = pair
        product = lax.dot_general(left_side.astype(jnp.float32), table_rows.astype(jnp.float32), (((0,), (0,)), ((), ())), preferred_element_type=jnp.float32)
        return product.astype(jnp.bfloat16)
    coeffs = lax.map(one_mode, (per_mode, legendre)).reshape(M, NCHAN, KMAPS, 2, L)
    widened = coeffs.astype(jnp.float32)
    multiplier = jnp.where(mode_values > 0, 2.0, 1.0).astype(jnp.float32)
    per_ell = jnp.einsum('sikcl,sjkcl->ijl', widened * multiplier[:, None, None, None, None], widened, precision=lax.Precision.HIGHEST)
    bin_ends = jnp.cumsum(bin_widths).astype(jnp.int32)
    begins = bin_ends - bin_widths
    ell_values = jnp.arange(L, dtype=jnp.int32)
    onehot = ((ell_values[:, None] >= begins[None, :]) & (ell_values[:, None] < bin_ends[None, :])).astype(jnp.float32)
    binned = jnp.dot(per_ell.reshape(NCHAN * NCHAN, L), onehot, precision=lax.Precision.HIGHEST)
    spectra = binned.T.reshape(NBINS, NCHAN, NCHAN)
    weights = ilc_weights(spectra)
    per_ell_weights = jnp.dot(onehot, weights, precision=lax.Precision.HIGHEST)
    return jnp.einsum('sikcl,li->kcsl', widened, per_ell_weights, precision=lax.Precision.HIGHEST)
```

```python
import functools
import math

import jax
import jax.numpy as jnp
from jax import lax
from jax.experimental import pallas as pl
from jax.experimental.pallas import tpu as pltpu
from jax.sharding import PartitionSpec as P

F32 = jnp.float32
BF16 = jnp.bfloat16
PIX = 8192
PAIRS = [(i, j) for i in range(8) for j in range(i, 8)]
PROWS = 40
MESH = pl.DeviceIdType.MESH
VMEM = pltpu.VMEM
DMA = pltpu.SemaphoreType.DMA


def vspec():
    return pl.BlockSpec(memory_space=pltpu.VMEM)


def split_dot(a, b, dims):
    hi = a.astype(BF16)
    rest = a - hi.astype(F32)
    mid = rest.astype(BF16)
    low = (rest - mid.astype(F32)).astype(BF16)
    out = lax.dot_general(low, b, dims, preferred_element_type=F32)
    out += lax.dot_general(mid, b, dims, preferred_element_type=F32)
    return out + lax.dot_general(hi, b, dims, preferred_element_type=F32)


NN = (((1,), (0,)), ((), ()))
NT = (((1,), (1,)), ((), ()))


def swap_blocks(arrays, width):
    count = len(arrays)
    block = lax.broadcasted_iota(jnp.int32, arrays[0].shape, 1) // width
    arrays = list(arrays)
    step = 1
    while step < count:
        low = (block // step) % 2 == 0
        for i in range(count):
            if i & step:
                continue
            a, b = arrays[i], arrays[i | step]
            arrays[i] = jnp.where(low, a, pltpu.roll(b, step * width, 1))
            arrays[i | step] = jnp.where(low, pltpu.roll(a, 128 - step * width, 1), b)
        step *= 2
    return arrays


CHUNKS = 16


def sky_copy(x_hbm, xbuf, sem, n):
    width = PIX // CHUNKS
    return pltpu.make_async_copy(
        x_hbm.at[:, pl.ds(pl.multiple_of(n * width, width), width)], xbuf.at[n], sem.at[n]
    )


def fourier_part(m_ref, x_hbm, sb_ref, xbuf, tab_a, tab_b, rows, sem):
    lax.fori_loop(0, CHUNKS, lambda n, _: (sky_copy(x_hbm, xbuf, sem, n).start(), 0)[1], 0)
    m = m_ref[...]
    step = jnp.float32(2.0 * math.pi / PIX)
    high = lax.broadcasted_iota(jnp.int32, (64, 256), 0)
    quarter = (lax.broadcasted_iota(jnp.int32, (64, 256), 1) // 8) % 2 * (PIX // 4)
    ang = (((high * m) % 64 * 128 + quarter) % PIX).astype(F32) * step
    factor = jnp.float32(PIX ** (-0.5))
    tab_a[0] = jnp.cos(ang) * factor
    tab_a[1] = jnp.sin(ang) * factor
    low = lax.broadcasted_iota(jnp.int32, (128, 256), 0)
    ang = ((low * m) % PIX).astype(F32) * step
    tab_b[0] = jnp.cos(ang)
    tab_b[1] = jnp.sin(ang)
    rows[...] = jnp.zeros_like(rows)

    def chunk(n, _):
        parts = []
        for u in range(4):
            ca = tab_a[0, pl.ds(n * 4 + u, 1), :]
            sa = tab_a[1, pl.ds(n * 4 + u, 1), :]
            parts.append((tab_b[0] * ca - tab_b[1] * sa).astype(BF16))
        table = jnp.concatenate(parts, axis=0)
        sky_copy(x_hbm, xbuf, sem, n).wait()
        out = jnp.dot(xbuf[n], table, preferred_element_type=F32)
        rows[0] += out[:, :128]
        rows[1] += out[:, 128:]
        return 0

    lax.fori_loop(0, CHUNKS, chunk, 0)

    for xg in range(4):
        for half in range(2):
            parts = [rows[half, pl.ds(xg * 8 + k, 16, stride=32), :] for k in range(8)]
            for g, part in enumerate(swap_blocks(parts, 16)):
                sb_ref[xg, half * 8 + g] = part.astype(BF16)


def fourier_kernel(m_ref, x_hbm, sb_ref, xbuf, tab_a, tab_b, rows, sem):
    fourier_part(m_ref, x_hbm, sb_ref, xbuf, tab_a, tab_b, rows, sem)


def fourier_call(mcol, sky):
    return pl.pallas_call(
        fourier_kernel,
        out_shape=jax.ShapeDtypeStruct((4, 16, 16, 128), BF16),
        in_specs=[vspec(), pl.BlockSpec(memory_space=pl.ANY)],
        out_specs=vspec(),
        scratch_shapes=[
            VMEM((CHUNKS, 512, PIX // CHUNKS), BF16),
            VMEM((2, 64, 256), F32),
            VMEM((2, 128, 256), F32),
            VMEM((2, 512, 128), F32),
            DMA((CHUNKS,)),
        ],
        compiler_params=pltpu.CompilerParams(vmem_limit_bytes=32 << 20),
        name="fourier",
    )(mcol, sky)


def place():
    freq = lax.axis_index("freq")
    blk = lax.axis_index("blk")
    return freq // 2, freq % 2, blk


def greet(peers):
    barrier = pltpu.get_barrier_semaphore()
    total = 0
    for count, peer in peers:
        total += count

        def one(d, _, peer=peer):
            pl.semaphore_signal(barrier, inc=1, device_id=peer(d), device_id_type=MESH)
            return 0

        lax.fori_loop(1, count + 1, one, 0)
    pl.semaphore_wait(barrier, total)


def plane_peer(x, c, b, d):
    q = (x * 16 + b + d) % 64
    return (q // 16 * 2 + c, q % 16)


def plane_copy(src, dst, send, recv, x, c, b, d):
    q = (x * 16 + b + d) % 64
    return pltpu.make_async_remote_copy(
        src_ref=src.at[q // 16, q % 16],
        dst_ref=dst.at[x, b],
        send_sem=send.at[d],
        recv_sem=recv.at[x * 16 + b],
        device_id=(q // 16 * 2 + c, q % 16),
        device_id_type=MESH,
    )


def plane_arrival(src, dst, send, recv, x, c, b, p):
    return pltpu.make_async_remote_copy(
        src_ref=src.at[p // 16, p % 16],
        dst_ref=dst.at[p // 16, p % 16],
        send_sem=send.at[0],
        recv_sem=recv.at[p],
        device_id=(x * 2 + c, b),
        device_id_type=MESH,
    )


def plane_start(src, dst, send, recv, own, x, c, b):
    pltpu.make_async_copy(src.at[x, b], dst.at[x, b], own).start()

    def one(d, _):
        plane_copy(src, dst, send, recv, x, c, b, d).start()
        return 0

    lax.fori_loop(1, 64, one, 0)


def plane_send_wait(src, dst, send, recv, x, c, b):
    def one(d, _):
        plane_copy(src, dst, send, recv, x, c, b, d).wait_send()
        return 0

    lax.fori_loop(1, 64, one, 0)


def modes_exchange(sb_ref, rb_ref, send, recv, own, fsend, frecv):
    x, c, b = place()
    mine = rb_ref.at[c]
    theirs = rb_ref.at[1 - c]
    plane_start(sb_ref, mine, send, recv, own, x, c, b)
    pltpu.make_async_copy(sb_ref.at[x, b], mine.at[x, b], own).wait()

    def forward(g):
        return pltpu.make_async_remote_copy(
            src_ref=mine.at[g],
            dst_ref=mine.at[g],
            send_sem=fsend.at[g],
            recv_sem=frecv.at[g],
            device_id=(x * 2 + 1 - c, b),
            device_id_type=MESH,
        )

    def group(i, _):
        g = (x + i) % 4

        def one(j, _):
            p = g * 16 + j

            @pl.when(p != x * 16 + b)
            def _():
                plane_arrival(sb_ref, mine, send, recv, x, c, b, p).wait_recv()

            return 0

        lax.fori_loop(0, 16, one, 0)
        forward(g).start()
        return 0

    lax.fori_loop(0, 4, group, 0)
    plane_send_wait(sb_ref, mine, send, recv, x, c, b)

    def finish(g, _):
        forward(g).wait_send()
        pltpu.make_async_remote_copy(
            src_ref=theirs.at[g],
            dst_ref=theirs.at[g],
            send_sem=fsend.at[g],
            recv_sem=frecv.at[g],
            device_id=(x * 2 + 1 - c, b),
            device_id_type=MESH,
        ).wait_recv()
        return 0

    lax.fori_loop(0, 4, finish, 0)


def modes_kernel(sb_ref, rb_ref, send, recv, own, fsend, frecv):
    x, c, b = place()
    greet([
        (63, lambda d: plane_peer(x, c, b, d)),
        (1, lambda d: (x * 2 + 1 - c, b)),
    ])
    modes_exchange(sb_ref, rb_ref, send, recv, own, fsend, frecv)


def modes_call(sb):
    return pl.pallas_call(
        modes_kernel,
        out_shape=jax.ShapeDtypeStruct((2, 4, 16, 16, 128), BF16),
        in_specs=[vspec()],
        out_specs=vspec(),
        scratch_shapes=[DMA((64,)), DMA((64,)), DMA, DMA((4,)), DMA((4,))],
        compiler_params=pltpu.CompilerParams(collective_id=0, has_side_effects=True),
        name="modes_exchange",
    )(sb)


def sum_over_devices(part, got, send, recv):
    x, c, b = place()
    y, z = b // 4, b % 4
    stages = [
        (3, lambda d: (x * 2 + c, y * 4 + (z + d) % 4)),
        (3, lambda d: (x * 2 + c, (y + d) % 4 * 4 + z)),
        (3, lambda d: ((x + d) % 4 * 2 + c, b)),
        (1, lambda d: (x * 2 + 1 - c, b)),
    ]
    base = 0
    for index, (count, peer) in enumerate(stages):
        copies = []
        for d in range(1, count + 1):
            copies.append(
                pltpu.make_async_remote_copy(
                    src_ref=part.at[index],
                    dst_ref=got.at[base + d - 1],
                    send_sem=send.at[base + d - 1],
                    recv_sem=recv.at[base + d - 1],
                    device_id=peer(d),
                    device_id_type=MESH,
                )
            )
        for copy in copies:
            copy.start()
        total = part[index]
        for d, copy in enumerate(copies):
            copy.wait_recv()
            total = total + got[base + d]
        part[index + 1] = total
        for copy in copies:
            copy.wait_send()
        base += count


def sum_peers():
    x, c, b = place()
    y, z = b // 4, b % 4
    return [
        (3, lambda d: (x * 2 + c, y * 4 + (z + d) % 4)),
        (3, lambda d: (x * 2 + c, (y + d) % 4 * 4 + z)),
        (3, lambda d: ((x + d) % 4 * 2 + c, b)),
        (1, lambda d: (x * 2 + 1 - c, b)),
    ]


def solve_bins(packed, matrix):
    for row, (i, j) in enumerate(PAIRS):
        value = packed[pl.ds(row, 1), :]
        matrix[j, pl.ds(i, 1), :] = value
        if i != j:
            matrix[i, pl.ds(j, 1), :] = value
    columns = [matrix[j] for j in range(8)]
    rows = lax.broadcasted_iota(jnp.int32, (8, 128), 0)
    trace = sum(columns[j][j : j + 1] for j in range(8))
    load = jnp.float32(0.1) * trace / jnp.float32(8)
    columns = [columns[j] + jnp.where(rows == j, load, 0.0) for j in range(8)]
    z = jnp.ones((8, 128), F32)
    for j in range(8):
        pivot = columns[j][j : j + 1]
        scale = columns[j] / pivot
        keep = rows == j
        for k in range(j + 1, 8):
            columns[k] = columns[k] - jnp.where(keep, 0.0, scale * columns[k][j : j + 1])
        z = z - jnp.where(keep, 0.0, scale * z[j : j + 1])
        columns[j] = jnp.where(keep, columns[j], 0.0)
    diagonal = sum(columns)
    z = z / diagonal
    return z / jnp.sum(z, axis=0, keepdims=True)


def weights_kernel(sp_ref, w_ref, part, got, matrix, send, recv):
    greet(sum_peers())
    part[0] = sp_ref[...]
    sum_over_devices(part, got, send, recv)
    w_ref[...] = solve_bins(part.at[4], matrix)


def weights_call(sp):
    return pl.pallas_call(
        weights_kernel,
        out_shape=jax.ShapeDtypeStruct((8, 128), F32),
        in_specs=[vspec()],
        out_specs=vspec(),
        scratch_shapes=[
            VMEM((5, PROWS, 128), F32),
            VMEM((10, PROWS, 128), F32),
            VMEM((8, 8, 128), F32),
            DMA((10,)),
            DMA((10,)),
        ],
        compiler_params=pltpu.CompilerParams(collective_id=1, has_side_effects=True),
        name="weights",
    )(sp)


def bands_kernel(sb_ref, rb_ref, send, recv, own):
    x, c, b = place()
    greet([(63, lambda d: plane_peer(x, c, b, d))])
    plane_start(sb_ref, rb_ref, send, recv, own, x, c, b)
    pltpu.make_async_copy(sb_ref.at[x, b], rb_ref.at[x, b], own).wait()

    def one(d, _):
        p = (x * 16 + b + 64 - d) % 64
        plane_arrival(sb_ref, rb_ref, send, recv, x, c, b, p).wait_recv()
        return 0

    lax.fori_loop(1, 64, one, 0)
    plane_send_wait(sb_ref, rb_ref, send, recv, x, c, b)


def bands_call(sb):
    return pl.pallas_call(
        bands_kernel,
        out_shape=jax.ShapeDtypeStruct((4, 16, 32, 128), BF16),
        in_specs=[vspec()],
        out_specs=vspec(),
        scratch_shapes=[DMA((64,)), DMA((64,)), DMA],
        compiler_params=pltpu.CompilerParams(collective_id=2, has_side_effects=True),
        name="bands_exchange",
    )(sb)


def legendre_copy(leg_hbm, leg, sem, c, i):
    start = pl.multiple_of((i % 4 * 2 + c) * 512, 512)
    return pltpu.make_async_copy(
        leg_hbm.at[i // 4, :, pl.ds(start, 512)], leg.at[i // 4, i % 4], sem.at[i]
    )


def bin_rows(widths_ref, c, onehot):
    row = lax.broadcasted_iota(jnp.int32, (128, 128), 0)
    col = lax.broadcasted_iota(jnp.int32, (128, 128), 1)
    upper = jnp.where(row <= col, 1.0, 0.0).astype(BF16)
    widths = widths_ref[...].astype(F32)
    ends = split_dot(widths, upper, NN)
    begins = ends - widths
    ends, begins = ends[0:1], begins[0:1]

    def chunk(g, _):
        ell = lax.broadcasted_iota(jnp.int32, (512, 128), 0) + ((g * 2 + c) * 512)
        ell = ell.astype(F32)
        hit = jnp.where(ell >= begins, 1.0, 0.0) * jnp.where(ell < ends, 1.0, 0.0)
        onehot[pl.ds(pl.multiple_of(g * 512, 512), 512), :] = hit.astype(BF16)
        return 0

    lax.fori_loop(0, 4, chunk, 0)


def order_rows(rb, order_ref, left, turned):
    q = lax.broadcasted_iota(jnp.int32, (256, 256), 0)
    perm = jnp.where(q == order_ref[...], 1.0, 0.0).astype(BF16)

    def channel(ch, _):
        block = rb[ch % 2, ch // 2]
        sorted_rows = jnp.dot(perm, block, preferred_element_type=F32)
        for h in range(2):
            turned[h] = sorted_rows[h * 128 : h * 128 + 128].T
            for s in range(8):
                left[s, pl.ds(pl.multiple_of(ch * 16, 16), 16), h * 128 : h * 128 + 128] = turned[
                    h, pl.ds(s, 16, stride=8), :
                ].astype(BF16)
        return 0

    lax.fori_loop(0, 8, channel, 0)


def legendre_sums(leg_hbm, leg, sem, c, left, coef):
    def one(i, _):
        legendre_copy(leg_hbm, leg, sem, c, i).wait()
        out = jnp.dot(left[i // 4], leg[i // 4, i % 4], preferred_element_type=F32)
        coef[i // 4, :, pl.ds(pl.multiple_of(i % 4 * 512, 512), 512)] = out.astype(BF16)
        return 0

    lax.fori_loop(0, 32, one, 0)


def cross_spectra(coef, mult, sums, per_ell):
    def tile(t, _):
        lanes = pl.ds(pl.multiple_of(t * 128, 128), 128)
        acc = [jnp.zeros((8, 128), F32) for _ in PAIRS]

        def slot(s, acc):
            acc = list(acc)
            for half in range(1):
                values = [coef[s, i * 16 : i * 16 + 16, lanes].astype(F32) for i in range(8)]
                factor = mult(s)
                scaled = [v * factor for v in values]
                for n, (i, j) in enumerate(PAIRS):
                    prod = scaled[i] * values[j]
                    acc[n] = acc[n] + (prod[0:8] + prod[8:16])
            return tuple(acc)

        acc = lax.fori_loop(0, 8, slot, tuple(acc))
        for n, value in enumerate(acc):
            sums[n * 8 : n * 8 + 8, :] = value
        total = sums[pl.ds(0, PROWS, stride=8), :]
        for r in range(1, 8):
            total = total + sums[pl.ds(r, PROWS, stride=8), :]
        per_ell[:, lanes] = total
        return 0

    sums[...] = jnp.zeros_like(sums)
    lax.fori_loop(0, 16, tile, 0)


def slot_mult(mv_ref, b):
    return lambda s: (1 + jnp.minimum(mv_ref[b * 8 + s], 1)).astype(F32)


def spectra_kernel(mv_ref, order_ref, widths_ref, rb_ref, leg_hbm, coef_ref, sp_ref, onehot_ref, leg, left, turned, sums, per_ell, sem):
    x, c, b = place()
    lax.fori_loop(0, 32, lambda i, _: (legendre_copy(leg_hbm, leg, sem, c, i).start(), 0)[1], 0)
    bin_rows(widths_ref, c, onehot_ref)
    order_rows(rb_ref, order_ref, left, turned)
    legendre_sums(leg_hbm, leg, sem, c, left, coef_ref)
    cross_spectra(coef_ref, slot_mult(mv_ref, b), sums, per_ell)
    sp_ref[...] = split_dot(per_ell[...], onehot_ref[...], NN)


def spectra_call(mv, order, widths, rb, leg):
    return pl.pallas_call(
        spectra_kernel,
        out_shape=(
            jax.ShapeDtypeStruct((8, 128, 2048), BF16),
            jax.ShapeDtypeStruct((PROWS, 128), F32),
            jax.ShapeDtypeStruct((2048, 128), BF16),
        ),
        in_specs=[
            pl.BlockSpec(memory_space=pltpu.SMEM),
            vspec(),
            vspec(),
            vspec(),
            pl.BlockSpec(memory_space=pl.ANY),
        ],
        out_specs=(vspec(), vspec(), vspec()),
        scratch_shapes=[
            VMEM((8, 4, 256, 512), BF16),
            VMEM((8, 128, 256), BF16),
            VMEM((2, 128, 128), F32),
            VMEM((PROWS * 8, 128), F32),
            VMEM((PROWS, 2048), F32),
            DMA((32,)),
        ],
        compiler_params=pltpu.CompilerParams(vmem_limit_bytes=40 << 20),
        name="spectra",
    )(mv, order, widths, rb, leg)


def weighted_sums(coef, weights, onehot, table, turned, sb):
    table[...] = split_dot(weights, onehot[...], NT)

    def tile(t, _):
        lanes = pl.ds(pl.multiple_of(t * 128, 128), 128)
        per = [jnp.broadcast_to(table[i : i + 1, lanes], (16, 128)) for i in range(8)]
        for s in range(8):
            total = per[0] * coef[s, 0:16, lanes].astype(F32)
            for i in range(1, 8):
                total += per[i] * coef[s, i * 16 : i * 16 + 16, lanes].astype(F32)
            turned[pl.ds(s, 16, stride=8), :] = total
        out = turned[...].T.astype(BF16)
        for j in range(4):
            sb[t // 4, t % 4 * 4 + j] = out[j * 32 : j * 32 + 32]
        return 0

    lax.fori_loop(0, 16, tile, 0)


def clean_kernel(w_ref, onehot_ref, coef_ref, sb_ref, table, turned):
    weighted_sums(coef_ref, w_ref[...], onehot_ref, table, turned, sb_ref)


def clean_call(weights, onehot, coef):
    return pl.pallas_call(
        clean_kernel,
        out_shape=jax.ShapeDtypeStruct((4, 16, 32, 128), BF16),
        in_specs=[vspec(), vspec(), vspec()],
        out_specs=vspec(),
        scratch_shapes=[VMEM((8, 2048), F32), VMEM((128, 128), F32)],
        compiler_params=pltpu.CompilerParams(vmem_limit_bytes=32 << 20),
        name="weighted_sums",
    )(weights, onehot, coef)


def layout_kernel(rb_ref, out_ref):
    def group(i, _):
        x, rows = i // 4, pl.ds(pl.multiple_of(i % 4 * 8, 8), 8)
        parts = [rb_ref[x, b, rows, :].astype(F32) for b in range(16)]
        for kc, part in enumerate(swap_blocks(parts, 8)):
            out_ref[x * 16 + kc, rows, :] = part
        return 0

    lax.fori_loop(0, 16, group, 0)


def layout_call(rb):
    return pl.pallas_call(
        layout_kernel,
        out_shape=jax.ShapeDtypeStruct((64, 32, 128), F32),
        in_specs=[vspec()],
        out_specs=vspec(),
        name="output_layout",
    )(rb)


def on_device(sky_maps, legendre, mode_values, cycle_order, bin_widths):
    sky = sky_maps.reshape(512, PIX)
    slots = mode_values.reshape(16, 1, 8)
    mcol = jnp.broadcast_to(slots, (16, 2, 8)).reshape(1, 256)
    order = cycle_order.reshape(1, 256)
    widths = jnp.broadcast_to(bin_widths.reshape(1, 128), (8, 128))
    sb = fourier_call(mcol, sky)
    rb = modes_call(sb).reshape(2, 4, 256, 128)
    coef, sp, onehot = spectra_call(mode_values, order, widths, rb, legendre)
    weights = weights_call(sp)
    sb = clean_call(weights, onehot, coef)
    out = layout_call(bands_call(sb))
    return out.reshape(32, 2, 32, 128).transpose(0, 1, 3, 2)


def solution(mesh):
    return jax.shard_map(
        on_device,
        mesh=mesh,
        in_specs=(P("freq", "blk", None, None), P("blk", None, None), P(), P(), P()),
        out_specs=P(None, None, None, ("freq", "blk")),
        check_vma=False,
    )
```

```python
import functools
import math

import jax
import jax.numpy as jnp
from jax import lax
from jax.experimental import pallas as pl
from jax.experimental.pallas import tpu as pltpu
from jax.sharding import PartitionSpec as P

F32 = jnp.float32
BF16 = jnp.bfloat16
PIX = 8192
PAIRS = [(i, j) for i in range(8) for j in range(i, 8)]
PROWS = 40
MESH = pl.DeviceIdType.MESH
VMEM = pltpu.VMEM
DMA = pltpu.SemaphoreType.DMA


def vspec():
    return pl.BlockSpec(memory_space=pltpu.VMEM)


def split_dot(a, b, dims):
    hi = a.astype(BF16)
    rest = a - hi.astype(F32)
    mid = rest.astype(BF16)
    low = (rest - mid.astype(F32)).astype(BF16)
    out = lax.dot_general(low, b, dims, preferred_element_type=F32)
    out += lax.dot_general(mid, b, dims, preferred_element_type=F32)
    return out + lax.dot_general(hi, b, dims, preferred_element_type=F32)


NN = (((1,), (0,)), ((), ()))
NT = (((1,), (1,)), ((), ()))


def swap_blocks(arrays, width):
    count = len(arrays)
    block = lax.broadcasted_iota(jnp.int32, arrays[0].shape, 1) // width
    arrays = list(arrays)
    step = 1
    while step < count:
        low = (block // step) % 2 == 0
        for i in range(count):
            if i & step:
                continue
            a, b = arrays[i], arrays[i | step]
            arrays[i] = jnp.where(low, a, pltpu.roll(b, step * width, 1))
            arrays[i | step] = jnp.where(low, pltpu.roll(a, 128 - step * width, 1), b)
        step *= 2
    return arrays


CHUNKS = 16


def sky_copy(x_hbm, xbuf, sem, n):
    width = PIX // CHUNKS
    return pltpu.make_async_copy(
        x_hbm.at[:, pl.ds(pl.multiple_of(n * width, width), width)], xbuf.at[n], sem.at[n]
    )


def fourier_part(m_ref, x_hbm, sb_ref, xbuf, tab_a, tab_b, rows, sem):
    lax.fori_loop(0, CHUNKS, lambda n, _: (sky_copy(x_hbm, xbuf, sem, n).start(), 0)[1], 0)
    m = m_ref[...]
    step = jnp.float32(2.0 * math.pi / PIX)
    high = lax.broadcasted_iota(jnp.int32, (64, 256), 0)
    quarter = (lax.broadcasted_iota(jnp.int32, (64, 256), 1) // 8) % 2 * (PIX // 4)
    ang = (((high * m) % 64 * 128 + quarter) % PIX).astype(F32) * step
    factor = jnp.float32(PIX ** (-0.5))
    tab_a[0] = jnp.cos(ang) * factor
    tab_a[1] = jnp.sin(ang) * factor
    low = lax.broadcasted_iota(jnp.int32, (128, 256), 0)
    ang = ((low * m) % PIX).astype(F32) * step
    tab_b[0] = jnp.cos(ang)
    tab_b[1] = jnp.sin(ang)
    rows[...] = jnp.zeros_like(rows)

    def chunk(n, _):
        parts = []
        for u in range(4):
            ca = tab_a[0, pl.ds(n * 4 + u, 1), :]
            sa = tab_a[1, pl.ds(n * 4 + u, 1), :]
            parts.append((tab_b[0] * ca - tab_b[1] * sa).astype(BF16))
        table = jnp.concatenate(parts, axis=0)
        sky_copy(x_hbm, xbuf, sem, n).wait()
        out = jnp.dot(xbuf[n], table, preferred_element_type=F32)
        rows[0] += out[:, :128]
        rows[1] += out[:, 128:]
        return 0

    lax.fori_loop(0, CHUNKS, chunk, 0)

    for xg in range(4):
        for half in range(2):
            parts = [rows[half, pl.ds(xg * 8 + k, 16, stride=32), :] for k in range(8)]
            for g, part in enumerate(swap_blocks(parts, 16)):
                sb_ref[xg, half * 8 + g] = part.astype(BF16)


def place():
    freq = lax.axis_index("freq")
    blk = lax.axis_index("blk")
    return freq // 2, freq % 2, blk


def plane_peer(x, c, b, d):
    q = (x * 16 + b + d) % 64
    return (q // 16 * 2 + c, q % 16)


def plane_copy(src, dst, send, recv, x, c, b, d):
    q = (x * 16 + b + d) % 64
    return pltpu.make_async_remote_copy(
        src_ref=src.at[q // 16, q % 16],
        dst_ref=dst.at[x, b],
        send_sem=send.at[d],
        recv_sem=recv.at[x * 16 + b],
        device_id=(q // 16 * 2 + c, q % 16),
        device_id_type=MESH,
    )


def plane_arrival(src, dst, send, recv, x, c, b, p):
    return pltpu.make_async_remote_copy(
        src_ref=src.at[p // 16, p % 16],
        dst_ref=dst.at[p // 16, p % 16],
        send_sem=send.at[0],
        recv_sem=recv.at[p],
        device_id=(x * 2 + c, b),
        device_id_type=MESH,
    )


def plane_start(src, dst, send, recv, own, x, c, b):
    pltpu.make_async_copy(src.at[x, b], dst.at[x, b], own).start()

    def one(d, _):
        plane_copy(src, dst, send, recv, x, c, b, d).start()
        return 0

    lax.fori_loop(1, 64, one, 0)


def plane_send_wait(src, dst, send, recv, x, c, b):
    def one(d, _):
        plane_copy(src, dst, send, recv, x, c, b, d).wait_send()
        return 0

    lax.fori_loop(1, 64, one, 0)


def forward_copy(rb, fsend, frecv, x, c, b, core, g):
    return pltpu.make_async_remote_copy(
        src_ref=rb.at[core, g],
        dst_ref=rb.at[core, g],
        send_sem=fsend.at[g],
        recv_sem=frecv.at[g],
        device_id=(x * 2 + 1 - c, b),
        device_id_type=MESH,
    )


def wait_group(src, dst, send, recv, x, c, b, g):
    def one(j, _):
        p = g * 16 + j

        @pl.when(p != x * 16 + b)
        def _():
            plane_arrival(src, dst, send, recv, x, c, b, p).wait_recv()

        return 0

    lax.fori_loop(0, 16, one, 0)


def sum_over_devices(part, got, send, recv):
    x, c, b = place()
    y, z = b // 4, b % 4
    stages = [
        (3, lambda d: (x * 2 + c, y * 4 + (z + d) % 4)),
        (3, lambda d: (x * 2 + c, (y + d) % 4 * 4 + z)),
        (3, lambda d: ((x + d) % 4 * 2 + c, b)),
        (1, lambda d: (x * 2 + 1 - c, b)),
    ]
    base = 0
    for index, (count, peer) in enumerate(stages):
        copies = []
        for d in range(1, count + 1):
            copies.append(
                pltpu.make_async_remote_copy(
                    src_ref=part.at[index],
                    dst_ref=got.at[base + d - 1],
                    send_sem=send.at[base + d - 1],
                    recv_sem=recv.at[base + d - 1],
                    device_id=peer(d),
                    device_id_type=MESH,
                )
            )
        for copy in copies:
            copy.start()
        total = part[index]
        for d, copy in enumerate(copies):
            copy.wait_recv()
            total = total + got[base + d]
        part[index + 1] = total
        for copy in copies:
            copy.wait_send()
        base += count


def solve_bins(packed, matrix):
    for row, (i, j) in enumerate(PAIRS):
        value = packed[pl.ds(row, 1), :]
        matrix[j, pl.ds(i, 1), :] = value
        if i != j:
            matrix[i, pl.ds(j, 1), :] = value
    columns = [matrix[j] for j in range(8)]
    rows = lax.broadcasted_iota(jnp.int32, (8, 128), 0)
    trace = sum(columns[j][j : j + 1] for j in range(8))
    load = jnp.float32(0.1) * trace / jnp.float32(8)
    columns = [columns[j] + jnp.where(rows == j, load, 0.0) for j in range(8)]
    z = jnp.ones((8, 128), F32)
    for j in range(8):
        pivot = columns[j][j : j + 1]
        scale = columns[j] / pivot
        keep = rows == j
        for k in range(j + 1, 8):
            columns[k] = columns[k] - jnp.where(keep, 0.0, scale * columns[k][j : j + 1])
        z = z - jnp.where(keep, 0.0, scale * z[j : j + 1])
        columns[j] = jnp.where(keep, columns[j], 0.0)
    diagonal = sum(columns)
    z = z / diagonal
    return z / jnp.sum(z, axis=0, keepdims=True)


def legendre_copy(leg_hbm, leg, sem, c, i):
    start = pl.multiple_of((i % 4 * 2 + c) * 512, 512)
    return pltpu.make_async_copy(
        leg_hbm.at[i // 4, :, pl.ds(start, 512)], leg.at[i // 4, i % 4], sem.at[i]
    )


def bin_rows(widths_ref, c, onehot):
    row = lax.broadcasted_iota(jnp.int32, (128, 128), 0)
    col = lax.broadcasted_iota(jnp.int32, (128, 128), 1)
    upper = jnp.where(row <= col, 1.0, 0.0).astype(BF16)
    widths = widths_ref[...].astype(F32)
    ends = split_dot(widths, upper, NN)
    begins = ends - widths
    ends, begins = ends[0:1], begins[0:1]

    def chunk(g, _):
        ell = lax.broadcasted_iota(jnp.int32, (512, 128), 0) + ((g * 2 + c) * 512)
        ell = ell.astype(F32)
        hit = jnp.where(ell >= begins, 1.0, 0.0) * jnp.where(ell < ends, 1.0, 0.0)
        onehot[pl.ds(pl.multiple_of(g * 512, 512), 512), :] = hit.astype(BF16)
        return 0

    lax.fori_loop(0, 4, chunk, 0)


def order_channel(rb, perm, left, turned, core, g):
    ch = g * 2 + core
    block = rb[core, g].reshape(256, 128)
    sorted_rows = jnp.dot(perm[...], block, preferred_element_type=F32)
    for h in range(2):
        turned[h] = sorted_rows[h * 128 : h * 128 + 128].T
        for s in range(8):
            left[s, pl.ds(pl.multiple_of(ch * 16, 16), 16), h * 128 : h * 128 + 128] = turned[
                h, pl.ds(s, 16, stride=8), :
            ].astype(BF16)


def legendre_sums(leg_hbm, leg, sem, c, left, coef):
    def one(i, _):
        legendre_copy(leg_hbm, leg, sem, c, i).wait()
        out = jnp.dot(left[i // 4], leg[i // 4, i % 4], preferred_element_type=F32)
        coef[i // 4, :, pl.ds(pl.multiple_of(i % 4 * 512, 512), 512)] = out.astype(BF16)
        return 0

    lax.fori_loop(0, 32, one, 0)


def cross_spectra(coef, mult, sums, per_ell):
    def tile(t, _):
        lanes = pl.ds(pl.multiple_of(t * 128, 128), 128)
        acc = [jnp.zeros((8, 128), F32) for _ in PAIRS]

        def slot(s, acc):
            acc = list(acc)
            for half in range(1):
                values = [coef[s, i * 16 : i * 16 + 16, lanes].astype(F32) for i in range(8)]
                factor = mult(s)
                scaled = [v * factor for v in values]
                for n, (i, j) in enumerate(PAIRS):
                    prod = scaled[i] * values[j]
                    acc[n] = acc[n] + (prod[0:8] + prod[8:16])
            return tuple(acc)

        acc = lax.fori_loop(0, 8, slot, tuple(acc))
        for n, value in enumerate(acc):
            sums[n * 8 : n * 8 + 8, :] = value
        total = sums[pl.ds(0, PROWS, stride=8), :]
        for r in range(1, 8):
            total = total + sums[pl.ds(r, PROWS, stride=8), :]
        per_ell[:, lanes] = total
        return 0

    sums[...] = jnp.zeros_like(sums)
    lax.fori_loop(0, 16, tile, 0)


def slot_mult(mv_ref, b):
    return lambda s: (1 + jnp.minimum(mv_ref[b * 8 + s], 1)).astype(F32)


def weighted_sums(coef, weights, onehot, table, turned, sb):
    table[...] = split_dot(weights, onehot[...], NT)

    def tile(t, _):
        lanes = pl.ds(pl.multiple_of(t * 128, 128), 128)
        per = [jnp.broadcast_to(table[i : i + 1, lanes], (16, 128)) for i in range(8)]
        for s in range(8):
            total = per[0] * coef[s, 0:16, lanes].astype(F32)
            for i in range(1, 8):
                total += per[i] * coef[s, i * 16 : i * 16 + 16, lanes].astype(F32)
            turned[pl.ds(s, 16, stride=8), :] = total
        parts = [turned[i * 32 : i * 32 + 32, :] for i in range(4)]
        for j, part in enumerate(swap_blocks(parts, 32)):
            sb[t // 4, t % 4 * 4 + j] = part.astype(BF16)
        return 0

    lax.fori_loop(0, 16, tile, 0)


def output_group(rb, out, x):
    for pair in range(2):
        parts = [rb[x, b, pair * 16 : pair * 16 + 16, :].astype(F32) for b in range(16)]
        for k in range(2):
            block = jnp.concatenate([p[k * 8 : k * 8 + 8] for p in parts], axis=0).T
            for i in range(4):
                out[x * 16 + i * 4 + pair * 2 + k] = block[i * 32 : i * 32 + 32]


def kernel(
    mv_ref, m_ref, order_ref, widths_ref, sky_hbm, leg_hbm, out_ref,
    xbuf, tab_a, tab_b, rows, sb1, rb1, perm, left, turned2, leg, coef, sums, per_ell,
    onehot, part, got, matrix, table, turned, sb3, rb3,
    sky_sem, leg_sem, send1, recv1, fsend, frecv, send2, recv2, send3, recv3, own,
):
    x, c, b = place()
    barrier = pltpu.get_barrier_semaphore()

    def hello(d, _):
        pl.semaphore_signal(barrier, device_id=plane_peer(x, c, b, d), device_id_type=MESH)
        return 0

    lax.fori_loop(1, 64, hello, 0)
    pl.semaphore_signal(barrier, device_id=(x * 2 + 1 - c, b), device_id_type=MESH)
    fourier_part(m_ref, sky_hbm, sb1, xbuf, tab_a, tab_b, rows, sky_sem)
    lax.fori_loop(0, 32, lambda i, _: (legendre_copy(leg_hbm, leg, leg_sem, c, i).start(), 0)[1], 0)

    pl.semaphore_wait(barrier, 64)
    mine = rb1.at[c]
    plane_start(sb1, mine, send1, recv1, own, x, c, b)
    bin_rows(widths_ref, c, onehot)
    q = lax.broadcasted_iota(jnp.int32, (256, 256), 0)
    perm[...] = jnp.where(q == order_ref[...], 1.0, 0.0).astype(BF16)
    pltpu.make_async_copy(sb1.at[x, b], mine.at[x, b], own).wait()

    def from_chips(i, _):
        g = (x + i) % 4
        wait_group(sb1, mine, send1, recv1, x, c, b, g)
        forward_copy(rb1, fsend, frecv, x, c, b, c, g).start()
        order_channel(rb1, perm, left, turned2, c, g)
        return 0

    lax.fori_loop(0, 4, from_chips, 0)

    def from_core(i, _):
        g = (x + i) % 4
        forward_copy(rb1, fsend, frecv, x, c, b, 1 - c, g).wait_recv()
        order_channel(rb1, perm, left, turned2, 1 - c, g)
        return 0

    lax.fori_loop(0, 4, from_core, 0)
    legendre_sums(leg_hbm, leg, leg_sem, c, left, coef)
    cross_spectra(coef, slot_mult(mv_ref, b), sums, per_ell)
    part[0] = split_dot(per_ell[...], onehot[...], NN)
    sum_over_devices(part, got, send2, recv2)
    weights = solve_bins(part.at[4], matrix)
    weighted_sums(coef, weights, onehot, table, turned, sb3)

    plane_start(sb3, rb3, send3, recv3, own, x, c, b)
    pltpu.make_async_copy(sb3.at[x, b], rb3.at[x, b], own).wait()

    def finish(i, _):
        g = (x + i) % 4
        wait_group(sb3, rb3, send3, recv3, x, c, b, g)
        output_group(rb3, out_ref, g)
        return 0

    lax.fori_loop(0, 4, finish, 0)
    plane_send_wait(sb1, mine, send1, recv1, x, c, b)
    lax.fori_loop(
        0, 4, lambda g, _: (forward_copy(rb1, fsend, frecv, x, c, b, c, g).wait_send(), 0)[1], 0
    )
    plane_send_wait(sb3, rb3, send3, recv3, x, c, b)


def on_device(sky_maps, legendre, mode_values, cycle_order, bin_widths):
    sky = sky_maps.reshape(512, PIX)
    slots = mode_values.reshape(16, 1, 8)
    mcol = jnp.broadcast_to(slots, (16, 2, 8)).reshape(1, 256)
    order = cycle_order.reshape(1, 256)
    widths = jnp.broadcast_to(bin_widths.reshape(1, 128), (8, 128))
    hbm = pl.BlockSpec(memory_space=pltpu.HBM)
    out = pl.pallas_call(
        kernel,
        out_shape=jax.ShapeDtypeStruct((64, 32, 128), F32),
        in_specs=[pl.BlockSpec(memory_space=pltpu.SMEM), vspec(), vspec(), vspec(), hbm, hbm],
        out_specs=vspec(),
        scratch_shapes=[
            VMEM((CHUNKS, 512, PIX // CHUNKS), BF16),
            VMEM((2, 64, 256), F32),
            VMEM((2, 128, 256), F32),
            VMEM((2, 512, 128), F32),
            VMEM((4, 16, 16, 128), BF16),
            VMEM((2, 4, 16, 16, 128), BF16),
            VMEM((256, 256), BF16),
            VMEM((8, 128, 256), BF16),
            VMEM((2, 128, 128), F32),
            VMEM((8, 4, 256, 512), BF16),
            VMEM((8, 128, 2048), BF16),
            VMEM((PROWS * 8, 128), F32),
            VMEM((PROWS, 2048), F32),
            VMEM((2048, 128), BF16),
            VMEM((5, PROWS, 128), F32),
            VMEM((10, PROWS, 128), F32),
            VMEM((8, 8, 128), F32),
            VMEM((8, 2048), F32),
            VMEM((128, 128), F32),
            VMEM((4, 16, 32, 128), BF16),
            VMEM((4, 16, 32, 128), BF16),
            DMA((CHUNKS,)),
            DMA((32,)),
            DMA((64,)),
            DMA((64,)),
            DMA((4,)),
            DMA((4,)),
            DMA((10,)),
            DMA((10,)),
            DMA((64,)),
            DMA((64,)),
            DMA,
        ],
        compiler_params=pltpu.CompilerParams(
            collective_id=0, has_side_effects=True, vmem_limit_bytes=48 << 20
        ),
        name="harmonic_ilc",
    )(mode_values, mcol, order, widths, sky, legendre)
    return out.reshape(32, 2, 32, 128).transpose(0, 1, 3, 2)


def solution(mesh):
    return jax.shard_map(
        on_device,
        mesh=mesh,
        in_specs=(P("freq", "blk", None, None), P("blk", None, None), P(), P(), P()),
        out_specs=P(None, None, None, ("freq", "blk")),
        check_vma=False,
    )
```

```python
import math

import jax
import jax.numpy as jnp
from jax import lax
from jax.experimental import pallas as pl
from jax.experimental.pallas import tpu as pltpu
from jax.sharding import PartitionSpec as P

F32 = jnp.float32
BF16 = jnp.bfloat16
PIX = 8192
CHUNKS = 16
WIDTH = PIX // CHUNKS
PAIRS = [(i, j) for i in range(8) for j in range(i, 8)]
PROWS = 40
PARTS = [(0, 16), (16, 16), (32, 8)]
MESH = pl.DeviceIdType.MESH
VMEM = pltpu.VMEM
DMA = pltpu.SemaphoreType.DMA
NN = (((1,), (0,)), ((), ()))
NT = (((1,), (1,)), ((), ()))


def hops(d):
    return min(d, 4 - d)


OFFSETS = sorted(((dy, dz) for dy in range(4) for dz in range(4)), key=lambda t: -hops(t[0]) - hops(t[1]))


def split_dot(a, b, dims):
    hi = a.astype(BF16)
    rest = a - hi.astype(F32)
    mid = rest.astype(BF16)
    low = (rest - mid.astype(F32)).astype(BF16)
    out = lax.dot_general(low, b, dims, preferred_element_type=F32)
    out += lax.dot_general(mid, b, dims, preferred_element_type=F32)
    return out + lax.dot_general(hi, b, dims, preferred_element_type=F32)


def swap_blocks(arrays, width):
    count = len(arrays)
    block = lax.broadcasted_iota(jnp.int32, arrays[0].shape, 1) // width
    arrays = list(arrays)
    step = 1
    while step < count:
        low = (block // step) % 2 == 0
        for i in range(count):
            if i & step:
                continue
            a, b = arrays[i], arrays[i | step]
            arrays[i] = jnp.where(low, a, pltpu.roll(b, step * width, 1))
            arrays[i | step] = jnp.where(low, pltpu.roll(a, 128 - step * width, 1), b)
        step *= 2
    return arrays


def turn(phase):
    quadrant = (phase + PIX // 8) // (PIX // 4)
    a = (phase - quadrant * (PIX // 4)).astype(F32) * jnp.float32(2.0 * math.pi / PIX)
    a2 = a * a
    s = jnp.float32(1 / 362880)
    for coefficient in (-1 / 5040, 1 / 120, -1 / 6, 1.0):
        s = s * a2 + jnp.float32(coefficient)
    s = s * a
    c = jnp.float32(-1 / 3628800)
    for coefficient in (1 / 40320, -1 / 720, 1 / 24, -1 / 2, 1.0):
        c = c * a2 + jnp.float32(coefficient)
    odd = quadrant % 2 == 1
    cosine = jnp.where(odd, s, c)
    sine = jnp.where(odd, c, s)
    cosine = jnp.where((quadrant + 1) % 4 >= 2, -cosine, cosine)
    sine = jnp.where(quadrant % 4 >= 2, -sine, sine)
    return cosine, sine


def wrap(v):
    return lax.rem(v, 4)


class Place:
    def __init__(self):
        freq = lax.axis_index("freq")
        self.b = lax.axis_index("blk")
        self.x, self.c = lax.div(freq, 2), lax.rem(freq, 2)
        self.y, self.z = lax.div(self.b, 4), lax.rem(self.b, 4)
        self.p = self.x * 16 + self.b
        self.partner = (self.x * 2 + 1 - self.c, self.b)

    def device(self, x, y, z):
        return (x * 2 + self.c, y * 4 + z)


def remote(src, dst, send, recv, device):
    return pltpu.make_async_remote_copy(
        src_ref=src, dst_ref=dst, send_sem=send, recv_sem=recv, device_id=device, device_id_type=MESH
    )


def wait_blocks(blocks, sem, count):
    part = blocks.at[pl.ds(0, count)]
    pltpu.make_async_copy(part, part, sem).wait()


def sky_copy(sky_hbm, xbuf, sem, n):
    return pltpu.make_async_copy(
        sky_hbm.at[:, pl.ds(pl.multiple_of(n * WIDTH, WIDTH), WIDTH)], xbuf.at[n], sem.at[n]
    )


def make_tables(modes, tab_a, tab_b):
    m = modes[...]
    factor = jnp.float32(PIX ** (-0.5))
    high = lax.broadcasted_iota(jnp.int32, (64, 128), 0)
    cosine, sine = turn((high * m) % 64 * 128)
    tab_a[0] = cosine * factor
    tab_a[1] = sine * factor
    low = lax.broadcasted_iota(jnp.int32, (128, 128), 0)
    cosine, sine = turn((low * m) % PIX)
    tab_b[0] = cosine
    tab_b[1] = sine


def make_chunk(tab_a, tab_b, table, n):
    for u in range(4):
        ca = tab_a[0, pl.ds(n * 4 + u, 1), :]
        sa = tab_a[1, pl.ds(n * 4 + u, 1), :]
        lines = slice(u * 128, u * 128 + 128)
        table[lines, 0:128] = (tab_b[0] * ca - tab_b[1] * sa).astype(BF16)
        table[lines, 128:256] = (tab_b[1] * (-ca) - tab_b[0] * sa).astype(BF16)


def fourier_rows(sky_hbm, xbuf, sem, tab_a, tab_b, table, rows):
    make_chunk(tab_a, tab_b, table.at[0], 0)
    rows[...] = jnp.zeros_like(rows)

    def chunk(n, _):
        sky_copy(sky_hbm, xbuf, sem, n).wait()
        now = lax.rem(n, 2)
        out = jnp.dot(xbuf[n], table[now], preferred_element_type=F32)
        make_chunk(tab_a, tab_b, table.at[1 - now], lax.rem(n + 1, CHUNKS))
        rows[0] += out[:, :128]
        rows[1] += out[:, 128:]
        return 0

    lax.fori_loop(0, CHUNKS, chunk, 0)


def legendre_copy(leg_hbm, leg, sem, c, u):
    start = (u // 2 * 2 + c) * 512 + u % 2 * 256
    return pltpu.make_async_copy(
        leg_hbm.at[:, :, pl.ds(pl.multiple_of(start, 256), 256)], leg.at[u], sem.at[u]
    )


def bin_columns(widths, c, onehot):
    row = lax.broadcasted_iota(jnp.int32, (128, 128), 0)
    col = lax.broadcasted_iota(jnp.int32, (128, 128), 1)
    upper = jnp.where(row <= col, 1.0, 0.0).astype(BF16)
    wide = jnp.broadcast_to(widths[...].astype(F32), (8, 128))
    ends = split_dot(wide, upper, NN)
    begins = ends - wide
    ends = jnp.broadcast_to(ends[0:1], (128, 128)).T
    begins = jnp.broadcast_to(begins[0:1], (128, 128)).T
    lane = lax.broadcasted_iota(jnp.int32, (128, 128), 1)

    def tile(t, _):
        ell = (lane + ((t // 4 * 2 + c) * 512 + t % 4 * 128)).astype(F32)
        hit = jnp.where(ell >= begins, 1.0, 0.0) * jnp.where(ell < ends, 1.0, 0.0)
        onehot[:, pl.ds(pl.multiple_of(t * 128, 128), 128)] = hit.astype(BF16)
        return 0

    lax.fori_loop(0, 16, tile, 0)


def mode_factors(modes, b, factors):
    lane = lax.broadcasted_iota(jnp.int32, (1, 128), 1)
    factor = (1 + jnp.minimum(modes[...], 1)).astype(F32)
    for s in range(8):
        one = jnp.sum(jnp.where(lane == b * 8 + s, factor, 0.0), axis=1, keepdims=True)
        factors[pl.ds(s, 1), :] = jnp.broadcast_to(one, (1, 128))


def order_channel(rb, perm, left, turned, core, g):
    ch = g * 2 + core
    block = rb[core, pl.ds(pl.multiple_of(g * 16, 16), 16)].reshape(256, 128)
    sorted_rows = jnp.dot(perm[...], block, preferred_element_type=F32)
    for h in range(2):
        turned[h] = sorted_rows[h * 128 : h * 128 + 128].T
    for h in range(2):
        for s in range(8):
            left[s, pl.ds(pl.multiple_of(ch * 16, 16), 16), h * 128 : h * 128 + 128] = turned[
                h, pl.ds(s, 16, stride=8), :
            ].astype(BF16)


def legendre_group(leg, left, coef, u):
    lanes = pl.ds(pl.multiple_of(u * 256, 256), 256)
    for s in range(8):
        out = jnp.dot(left[s], leg[u, s], preferred_element_type=F32)
        coef[s, :, lanes] = out.astype(BF16)


def spectra_group(coef, factors, sums, per_ell, onehot, total, u):
    for h in range(2):
        lanes = pl.ds(pl.multiple_of(u * 256 + h * 128, 128), 128)
        acc = [None] * len(PAIRS)
        for s in range(8):
            both = [coef[s, i * 16 : i * 16 + 16, lanes].astype(F32) for i in range(8)]
            factor = factors[pl.ds(s, 1), :]
            for half in range(2):
                values = [v[half * 8 : half * 8 + 8] for v in both]
                scaled = [v * factor for v in values]
                for n, (i, j) in enumerate(PAIRS):
                    product = scaled[i] * values[j]
                    acc[n] = product if acc[n] is None else acc[n] + product
        for n, value in enumerate(acc):
            sums[h, n * 8 : n * 8 + 8, :] = value
        line = sums[h, pl.ds(0, PROWS, stride=8), :]
        for r in range(1, 8):
            line = line + sums[h, pl.ds(r, PROWS, stride=8), :]
        per_ell[:, h * 128 : h * 128 + 128] = line
    group = pl.ds(pl.multiple_of(u * 256, 256), 256)
    total[...] += split_dot(per_ell[...], onehot[:, group], NT)


def legendre_spectra(leg_hbm, leg, sem, c, left, coef, factors, sums, per_ell, onehot, total):
    sums[...] = jnp.zeros_like(sums)
    total[...] = jnp.zeros_like(total)
    legendre_copy(leg_hbm, leg, sem, c, 0).wait()
    legendre_group(leg, left, coef, 0)

    def step(u, _):
        legendre_copy(leg_hbm, leg, sem, c, u + 1).wait()
        legendre_group(leg, left, coef, u + 1)
        spectra_group(coef, factors, sums, per_ell, onehot, total, u)
        return 0

    lax.fori_loop(0, 7, step, 0)
    spectra_group(coef, factors, sums, per_ell, onehot, total, 7)


def sum_over_devices(me, part, got, send, recv):
    x, y, z = me.x, me.y, me.z
    peers = [
        [me.device(x, y, wrap(z + d)) for d in (2, 1, 3)],
        [me.device(x, wrap(y + d), z) for d in (2, 1, 3)],
        [me.device(wrap(x + d), y, z) for d in (2, 1, 3)],
    ]
    started = []

    def go(stage, index):
        first, count = PARTS[index]
        lines = pl.ds(first, count)
        devices = peers[(stage + index) % 3] if stage < 3 else [me.partner]
        copies = []
        for d, device in enumerate(devices):
            n = (stage * 3 + index) * 3 + d
            copies.append(
                remote(
                    part.at[stage, lines], got.at[stage, d, lines], send.at[n], recv.at[n], device
                )
            )
            copies[-1].start()
        started.extend(copies)
        return copies

    flights = [go(0, index) for index in range(3)]
    for stage in range(4):
        later = []
        for index in range(3):
            first, count = PARTS[index]
            lines = pl.ds(first, count)
            value = part[stage, lines, :]
            for d, copy in enumerate(flights[index]):
                copy.wait_recv()
                value = value + got[stage, d, lines, :]
            part[stage + 1, lines, :] = value
            if stage < 3:
                later.append(go(stage + 1, index))
        flights = later
    return started


def solve_bins(packed, matrix):
    for row, (i, j) in enumerate(PAIRS):
        value = packed[pl.ds(row, 1), :]
        matrix[j, pl.ds(i, 1), :] = value
        if i != j:
            matrix[i, pl.ds(j, 1), :] = value
    columns = [matrix[j] for j in range(8)]
    rows = lax.broadcasted_iota(jnp.int32, (8, 128), 0)
    trace = sum(columns[j][j : j + 1] for j in range(8))
    load = jnp.float32(0.1) * trace / jnp.float32(8)
    columns = [columns[j] + jnp.where(rows == j, load, 0.0) for j in range(8)]
    z = jnp.ones((8, 128), F32)
    for j in range(8):
        pivot = columns[j][j : j + 1]
        scale = columns[j] / pivot
        keep = rows == j
        for k in range(j + 1, 8):
            columns[k] = columns[k] - jnp.where(keep, 0.0, scale * columns[k][j : j + 1])
        z = z - jnp.where(keep, 0.0, scale * z[j : j + 1])
        columns[j] = jnp.where(keep, columns[j], 0.0)
    z = z / sum(columns)
    return z / jnp.sum(z, axis=0, keepdims=True)


def weighted_tile(coef, table, turned, t):
    lanes = pl.ds(pl.multiple_of(t * 128, 128), 128)
    per = [jnp.broadcast_to(table[pl.ds(i, 1), lanes], (16, 128)) for i in range(8)]
    for s in range(8):
        total = per[0] * coef[s, 0:16, lanes].astype(F32)
        for i in range(1, 8):
            total += per[i] * coef[s, i * 16 : i * 16 + 16, lanes].astype(F32)
        turned[pl.ds(s, 16, stride=8), :] = total
    parts = [turned[i * 32 : i * 32 + 32, :] for i in range(4)]
    return swap_blocks(parts, 32)


def output_group(rb, out, x):
    for pair in range(2):
        parts = [rb[x * 16 + b, pair * 16 : pair * 16 + 16, :].astype(F32) for b in range(16)]
        for k in range(2):
            block = jnp.concatenate([p[k * 8 : k * 8 + 8] for p in parts], axis=0).T
            for i in range(4):
                out[x * 16 + i * 4 + pair * 2 + k] = block[i * 32 : i * 32 + 32]


def kernel(
    modes_hbm, order_hbm, widths_hbm, sky_hbm, leg_hbm, out_ref,
    modes, order, widths, xbuf, tab_a, tab_b, table, rows, sb1, rb1, perm, left, turned2, leg,
    coef, sums, per_ell, onehot, factors, part, got, matrix, spread, turned, sb3, rb3,
    small_sem, sky_sem, leg_sem, send1, recv1, fsend, frecv, send2, recv2, send3, recv3, own,
):
    me = Place()
    x, c, b = me.x, me.c, me.b
    small = [
        pltpu.make_async_copy(modes_hbm, modes, small_sem.at[0]),
        pltpu.make_async_copy(order_hbm, order, small_sem.at[1]),
        pltpu.make_async_copy(widths_hbm, widths, small_sem.at[2]),
    ]
    for copy in small:
        copy.start()
    for n in range(CHUNKS):
        sky_copy(sky_hbm, xbuf, sky_sem, n).start()
    for u in range(8):
        legendre_copy(leg_hbm, leg, leg_sem, c, u).start()
    barrier = pltpu.get_barrier_semaphore()
    for i in range(4):
        for dy, dz in OFFSETS:
            if i or dy or dz:
                device = me.device(wrap(x + i), wrap(me.y + dy), wrap(me.z + dz))
                pl.semaphore_signal(barrier, device_id=device, device_id_type=MESH)
    pl.semaphore_signal(barrier, device_id=me.partner, device_id_type=MESH)
    for copy in small:
        copy.wait()
    make_tables(modes, tab_a, tab_b)
    fourier_rows(sky_hbm, xbuf, sky_sem, tab_a, tab_b, table, rows)
    pl.semaphore_wait(barrier, 64)

    for i in (2, 1, 3, 0):
        xx = wrap(x + i)
        parts = [
            rows[half, pl.ds(xx * 8 + k, 16, stride=32), :] for k in range(8) for half in range(2)
        ]
        for g, block in enumerate(swap_blocks(parts, 8)):
            sb1[xx * 16 + g] = block.astype(BF16)
        for dy, dz in OFFSETS:
            if i or dy or dz:
                yy, zz = wrap(me.y + dy), wrap(me.z + dz)
                remote(
                    sb1.at[xx * 16 + yy * 4 + zz], rb1.at[c, me.p], send1, recv1.at[x],
                    me.device(xx, yy, zz),
                ).start()
    local = pltpu.make_async_copy(sb1.at[me.p], rb1.at[c, me.p], own)
    local.start()
    bin_columns(widths, c, onehot)
    mode_factors(modes, b, factors)
    q = lax.broadcasted_iota(jnp.int32, (256, 256), 0)
    perm[...] = jnp.where(q == order[...], 1.0, 0.0).astype(BF16)
    local.wait()

    def forward(core, g):
        lines = pl.ds(g * 16, 16)
        return remote(
            rb1.at[core, lines], rb1.at[core, lines], fsend.at[g], frecv.at[g], me.partner
        )

    for i in (2, 1, 3, 0):
        g = wrap(x + i)
        wait_blocks(rb1.at[c], recv1.at[g], 16 if i else 15)
        forward(c, g).start()
        order_channel(rb1, perm, left, turned2.at[0], c, g)
    for i in (2, 1, 3, 0):
        g = wrap(x + i)
        forward(1 - c, g).wait_recv()
        order_channel(rb1, perm, left, turned2.at[1], 1 - c, g)

    legendre_spectra(
        leg_hbm, leg, leg_sem, c, left, coef, factors, sums, per_ell, onehot, part.at[0]
    )
    started = sum_over_devices(me, part, got, send2, recv2)
    weights = solve_bins(part.at[4], matrix)
    spread[...] = split_dot(weights, onehot[...], NN)

    def tile(n, _):
        xx, yy = wrap(x + 1 + n // 4), wrap(me.y + 1 + n % 4)
        for zz, block in enumerate(
            weighted_tile(coef, spread, turned.at[lax.rem(n, 2)], xx * 4 + yy)
        ):
            sb3[xx * 16 + yy * 4 + zz] = block.astype(BF16)
        for zz in range(4):
            remote(
                sb3.at[xx * 16 + yy * 4 + zz], rb3.at[me.p], send3, recv3.at[x],
                me.device(xx, yy, zz),
            ).start()
        return 0

    lax.fori_loop(0, 15, tile, 0)
    for zz, block in enumerate(weighted_tile(coef, spread, turned.at[1], x * 4 + me.y)):
        sb3[x * 16 + me.y * 4 + zz] = block.astype(BF16)
    for d in (2, 1, 3):
        zz = wrap(me.z + d)
        remote(
            sb3.at[x * 16 + me.y * 4 + zz], rb3.at[me.p], send3, recv3.at[x],
            me.device(x, me.y, zz),
        ).start()
    local = pltpu.make_async_copy(sb3.at[me.p], rb3.at[me.p], own)
    local.start()
    for copy in started:
        copy.wait_send()
    for g in range(4):
        forward(c, g).wait_send()
    wait_blocks(sb1, send1, 63)
    local.wait()
    for i in (3, 2, 1, 0):
        g = wrap(x + i)
        wait_blocks(rb3, recv3.at[g], 16 if i else 15)
        output_group(rb3, out_ref, g)
    wait_blocks(sb3, send3, 63)


def on_device(sky_maps, legendre, mode_values, cycle_order, bin_widths):
    hbm = pl.BlockSpec(memory_space=pltpu.HBM)
    out = pl.pallas_call(
        kernel,
        out_shape=jax.ShapeDtypeStruct((64, 32, 128), F32),
        in_specs=[hbm] * 5,
        out_specs=pl.BlockSpec(memory_space=pltpu.VMEM),
        scratch_shapes=[
            VMEM((1, 128), jnp.int32),
            VMEM((1, 256), jnp.int32),
            VMEM((1, 128), jnp.int32),
            VMEM((CHUNKS, 512, WIDTH), BF16),
            VMEM((2, 64, 128), F32),
            VMEM((2, 128, 128), F32),
            VMEM((2, WIDTH, 256), BF16),
            VMEM((2, 512, 128), F32),
            VMEM((64, 16, 128), BF16),
            VMEM((2, 64, 16, 128), BF16),
            VMEM((256, 256), BF16),
            VMEM((8, 128, 256), BF16),
            VMEM((2, 2, 128, 128), F32),
            VMEM((8, 8, 256, 256), BF16),
            VMEM((8, 128, 2048), BF16),
            VMEM((2, PROWS * 8, 128), F32),
            VMEM((PROWS, 256), F32),
            VMEM((128, 2048), BF16),
            VMEM((8, 128), F32),
            VMEM((5, PROWS, 128), F32),
            VMEM((4, 3, PROWS, 128), F32),
            VMEM((8, 8, 128), F32),
            VMEM((8, 2048), F32),
            VMEM((2, 128, 128), F32),
            VMEM((64, 32, 128), BF16),
            VMEM((64, 32, 128), BF16),
            DMA((3,)),
            DMA((CHUNKS,)),
            DMA((8,)),
            DMA,
            DMA((4,)),
            DMA((4,)),
            DMA((4,)),
            DMA((36,)),
            DMA((36,)),
            DMA,
            DMA((4,)),
            DMA,
        ],
        compiler_params=pltpu.CompilerParams(
            collective_id=0, has_side_effects=True, vmem_limit_bytes=48 << 20
        ),
        name="harmonic_ilc",
    )(
        mode_values.reshape(1, 128),
        cycle_order.reshape(1, 256),
        bin_widths.reshape(1, 128),
        sky_maps.reshape(512, PIX),
        legendre,
    )
    return out.reshape(32, 2, 32, 128).transpose(0, 1, 3, 2)


def solution(mesh):
    return jax.shard_map(
        on_device,
        mesh=mesh,
        in_specs=(P("freq", "blk", None, None), P("blk", None, None), P(), P(), P()),
        out_specs=P(None, None, None, ("freq", "blk")),
        check_vma=False,
    )
```

```python
import math

import jax
import jax.numpy as jnp
from jax import lax
from jax.experimental import pallas as pl
from jax.experimental.pallas import tpu as pltpu
from jax.sharding import PartitionSpec as P

F32 = jnp.float32
BF16 = jnp.bfloat16
PIX = 8192
CHUNKS = 4
TURNS = PIX // CHUNKS // 128
WIDTH = PIX // CHUNKS
PAIRS = [(i, j) for i in range(8) for j in range(i, 8)]
PROWS = 40
PARTS = [(0, 16), (16, 16), (32, 8)]
MESH = pl.DeviceIdType.MESH
VMEM = pltpu.VMEM
DMA = pltpu.SemaphoreType.DMA
NN = (((1,), (0,)), ((), ()))
NT = (((1,), (1,)), ((), ()))


def hops(d):
    return min(d, 4 - d)


OFFSETS = sorted(((dy, dz) for dy in range(4) for dz in range(4)), key=lambda t: -hops(t[0]) - hops(t[1]))


def split_dot(a, b, dims):
    hi = a.astype(BF16)
    rest = a - hi.astype(F32)
    mid = rest.astype(BF16)
    low = (rest - mid.astype(F32)).astype(BF16)
    out = lax.dot_general(low, b, dims, preferred_element_type=F32)
    out += lax.dot_general(mid, b, dims, preferred_element_type=F32)
    return out + lax.dot_general(hi, b, dims, preferred_element_type=F32)


def swap_blocks(arrays, width):
    count = len(arrays)
    block = lax.broadcasted_iota(jnp.int32, arrays[0].shape, 1) // width
    arrays = list(arrays)
    step = 1
    while step < count:
        low = (block // step) % 2 == 0
        for i in range(count):
            if i & step:
                continue
            a, b = arrays[i], arrays[i | step]
            arrays[i] = jnp.where(low, a, pltpu.roll(b, step * width, 1))
            arrays[i | step] = jnp.where(low, pltpu.roll(a, 128 - step * width, 1), b)
        step *= 2
    return arrays


def turn(phase):
    quadrant = jnp.right_shift(phase + PIX // 8, 11)
    a = (phase - jnp.left_shift(quadrant, 11)).astype(F32) * jnp.float32(2.0 * math.pi / PIX)
    a2 = a * a
    s = jnp.float32(1 / 362880)
    for coefficient in (-1 / 5040, 1 / 120, -1 / 6, 1.0):
        s = s * a2 + jnp.float32(coefficient)
    s = s * a
    c = jnp.float32(-1 / 3628800)
    for coefficient in (1 / 40320, -1 / 720, 1 / 24, -1 / 2, 1.0):
        c = c * a2 + jnp.float32(coefficient)
    odd = (quadrant & 1) == 1
    cosine = jnp.where(odd, s, c)
    sine = jnp.where(odd, c, s)
    cosine = jnp.where(((quadrant + 1) & 2) == 2, -cosine, cosine)
    sine = jnp.where((quadrant & 2) == 2, -sine, sine)
    return cosine, sine


def wrap(v):
    return lax.rem(v, 4)


class Place:
    def __init__(self):
        freq = lax.axis_index("freq")
        self.b = lax.axis_index("blk")
        self.x, self.c = lax.div(freq, 2), lax.rem(freq, 2)
        self.y, self.z = lax.div(self.b, 4), lax.rem(self.b, 4)
        self.p = self.x * 16 + self.b
        self.partner = (self.x * 2 + 1 - self.c, self.b)

    def device(self, x, y, z, core=None):
        return (x * 2 + (self.c if core is None else core), y * 4 + z)

    def along(self, core=None):
        x, y, z = self.x, self.y, self.z
        return [
            [self.device(x, y, wrap(z + d), core) for d in (2, 1, 3)],
            [self.device(x, wrap(y + d), z, core) for d in (2, 1, 3)],
            [self.device(wrap(x + d), y, z, core) for d in (2, 1, 3)],
        ]


def remote(src, dst, send, recv, device):
    return pltpu.make_async_remote_copy(
        src_ref=src, dst_ref=dst, send_sem=send, recv_sem=recv, device_id=device, device_id_type=MESH
    )


def wait_blocks(blocks, sem, count):
    part = blocks.at[pl.ds(0, count)]
    pltpu.make_async_copy(part, part, sem).wait()


def sky_copy(sky_hbm, xbuf, sem, n):
    return pltpu.make_async_copy(
        sky_hbm.at[:, pl.ds(pl.multiple_of(n * WIDTH, WIDTH), WIDTH)], xbuf.at[n], sem.at[n]
    )


def make_tables(modes, tab_a, tab_b):
    m = modes[...]
    factor = jnp.float32(PIX ** (-0.5))
    high = lax.broadcasted_iota(jnp.int32, (64, 128), 0)
    cosine, sine = turn(jnp.left_shift((high * m) & 63, 7))
    tab_a[0] = cosine * factor
    tab_a[1] = sine * factor
    low = lax.broadcasted_iota(jnp.int32, (128, 128), 0)
    cosine, sine = turn((low * m) & (PIX - 1))
    tab_b[0] = cosine
    tab_b[1] = sine


def make_chunk(tab_a, tab_b, table, n):
    for u in range(TURNS):
        ca = tab_a[0, pl.ds(n * TURNS + u, 1), :]
        sa = tab_a[1, pl.ds(n * TURNS + u, 1), :]
        lines = slice(u * 128, u * 128 + 128)
        table[lines, 0:128] = (tab_b[0] * ca - tab_b[1] * sa).astype(BF16)
        table[lines, 128:256] = (tab_b[1] * (-ca) - tab_b[0] * sa).astype(BF16)


def fourier_rows(sky_hbm, xbuf, sem, tab_a, tab_b, table, rows):
    make_chunk(tab_a, tab_b, table.at[0], 0)
    rows[...] = jnp.zeros_like(rows)

    def chunk(n, _):
        sky_copy(sky_hbm, xbuf, sem, n).wait()
        now = lax.rem(n, 2)
        out = jnp.dot(xbuf[n], table[now], preferred_element_type=F32)
        make_chunk(tab_a, tab_b, table.at[1 - now], lax.rem(n + 1, CHUNKS))
        rows[0] += out[:, :128]
        rows[1] += out[:, 128:]
        return 0

    lax.fori_loop(0, CHUNKS, chunk, 0)


def legendre_copy(leg_hbm, leg, sem, c, u):
    start = (u // 2 * 2 + c) * 512 + u % 2 * 256
    return pltpu.make_async_copy(
        leg_hbm.at[:, :, pl.ds(pl.multiple_of(start, 256), 256)], leg.at[u], sem.at[u]
    )


def bin_columns(widths, c, onehot):
    row = lax.broadcasted_iota(jnp.int32, (128, 128), 0)
    col = lax.broadcasted_iota(jnp.int32, (128, 128), 1)
    upper = jnp.where(row <= col, 1.0, 0.0).astype(BF16)
    wide = jnp.broadcast_to(widths[...].astype(F32), (8, 128))
    ends = split_dot(wide, upper, NN)
    begins = ends - wide
    ends = jnp.broadcast_to(ends[0:1], (128, 128)).T
    begins = jnp.broadcast_to(begins[0:1], (128, 128)).T
    lane = lax.broadcasted_iota(jnp.int32, (128, 128), 1)

    def tile(t, _):
        ell = (lane + ((t // 4 * 2 + c) * 512 + t % 4 * 128)).astype(F32)
        hit = jnp.where(ell >= begins, 1.0, 0.0) * jnp.where(ell < ends, 1.0, 0.0)
        onehot[:, pl.ds(pl.multiple_of(t * 128, 128), 128)] = hit.astype(BF16)
        return 0

    lax.fori_loop(0, 16, tile, 0)


def mode_factors(modes, b, factors):
    lane = lax.broadcasted_iota(jnp.int32, (1, 128), 1)
    factor = (1 + jnp.minimum(modes[...], 1)).astype(F32)
    for s in range(8):
        one = jnp.sum(jnp.where(lane == b * 8 + s, factor, 0.0), axis=1, keepdims=True)
        factors[pl.ds(s, 1), :] = jnp.broadcast_to(one, (1, 128))


def order_channel(rb, perm, left, turned, core, g):
    ch = g * 2 + core
    block = rb[core, pl.ds(pl.multiple_of(g * 16, 16), 16)].reshape(256, 128)
    sorted_rows = jnp.dot(perm[...], block, preferred_element_type=F32)
    for h in range(2):
        turned[h] = sorted_rows[h * 128 : h * 128 + 128].T
    for h in range(2):
        for s in range(8):
            left[s, pl.ds(pl.multiple_of(ch * 16, 16), 16), h * 128 : h * 128 + 128] = turned[
                h, pl.ds(s, 16, stride=8), :
            ].astype(BF16)


def legendre_group(leg, left, coef, fresh, u):
    lanes = pl.ds(pl.multiple_of(u * 256, 256), 256)
    for s in range(8):
        out = jnp.dot(left[s], leg[u, s], preferred_element_type=F32).astype(BF16)
        fresh[s] = out
        coef[s, :, lanes] = out


def spectra_group(fresh, factors, sums, per_ell, onehot, total, u):
    for h in range(2):
        lanes = slice(h * 128, h * 128 + 128)
        acc = [None] * len(PAIRS)
        for s in range(8):
            both = [fresh[s, i * 16 : i * 16 + 16, lanes].astype(F32) for i in range(8)]
            factor = factors[pl.ds(s, 1), :]
            for half in range(2):
                values = [v[half * 8 : half * 8 + 8] for v in both]
                scaled = [v * factor for v in values]
                for n, (i, j) in enumerate(PAIRS):
                    product = scaled[i] * values[j]
                    acc[n] = product if acc[n] is None else acc[n] + product
        for n, value in enumerate(acc):
            sums[h, n * 8 : n * 8 + 8, :] = value
        line = sums[h, pl.ds(0, PROWS, stride=8), :]
        for r in range(1, 8):
            line = line + sums[h, pl.ds(r, PROWS, stride=8), :]
        per_ell[:, h * 128 : h * 128 + 128] = line
    group = pl.ds(pl.multiple_of(u * 256, 256), 256)
    total[...] += split_dot(per_ell[...], onehot[:, group], NT)


def legendre_spectra(
    leg_hbm, leg, sem, c, left, coef, even, odd, factors, sums, per_ell, onehot, total
):
    sums[...] = jnp.zeros_like(sums)
    total[...] = jnp.zeros_like(total)
    for u in range(8):
        legendre_copy(leg_hbm, leg, sem, c, u).wait()
    legendre_group(leg, left, coef, even, 0)

    def step(v, _):
        legendre_group(leg, left, coef, odd, v * 2 + 1)
        spectra_group(even, factors, sums.at[0], per_ell.at[0], onehot, total, v * 2)
        legendre_group(leg, left, coef, even, v * 2 + 2)
        spectra_group(odd, factors, sums.at[1], per_ell.at[1], onehot, total, v * 2 + 1)
        return 0

    lax.fori_loop(0, 3, step, 0)
    legendre_group(leg, left, coef, odd, 7)
    spectra_group(even, factors, sums.at[0], per_ell.at[0], onehot, total, 6)
    spectra_group(odd, factors, sums.at[1], per_ell.at[1], onehot, total, 7)


def sum_over_devices(me, part, got, send, recv):
    near, far = me.along(), me.along(1 - me.c)

    def go(stage, index):
        lines = pl.ds(*PARTS[index])
        axis = (stage + index) % 3
        devices = near[axis]
        if stage == 2:
            devices = near[axis] + far[axis] + [me.partner]
        for d, device in enumerate(devices):
            remote(
                part.at[stage, lines], got.at[stage * 7 + d, lines], send,
                recv.at[stage * 3 + index], device,
            ).start()
        return len(devices)

    counts = [go(0, index) for index in range(3)]
    for stage in range(3):
        later = []
        for index in range(3):
            lines = pl.ds(*PARTS[index])
            arrived = got.at[pl.ds(stage * 7, counts[index]), lines]
            pltpu.make_async_copy(arrived, arrived, recv.at[stage * 3 + index]).wait()
            value = part[stage, lines, :]
            for d in range(counts[index]):
                value = value + got[stage * 7 + d, lines, :]
            part[stage + 1, lines, :] = value
            if stage < 2:
                later.append(go(stage + 1, index))
        counts = later


def solve_bins(packed, matrix):
    for row, (i, j) in enumerate(PAIRS):
        value = packed[pl.ds(row, 1), :]
        matrix[j, pl.ds(i, 1), :] = value
        if i != j:
            matrix[i, pl.ds(j, 1), :] = value
    columns = [matrix[j] for j in range(8)]
    rows = lax.broadcasted_iota(jnp.int32, (8, 128), 0)
    trace = sum(columns[j][j : j + 1] for j in range(8))
    load = jnp.float32(0.1) * trace / jnp.float32(8)
    columns = [columns[j] + jnp.where(rows == j, load, 0.0) for j in range(8)]
    z = jnp.ones((8, 128), F32)
    for j in range(8):
        pivot = columns[j][j : j + 1]
        scale = columns[j] / pivot
        keep = rows == j
        for k in range(j + 1, 8):
            columns[k] = columns[k] - jnp.where(keep, 0.0, scale * columns[k][j : j + 1])
        z = z - jnp.where(keep, 0.0, scale * z[j : j + 1])
        columns[j] = jnp.where(keep, columns[j], 0.0)
    z = z / sum(columns)
    return z / jnp.sum(z, axis=0, keepdims=True)


def weighted_tile(coef, table, turned, t):
    lanes = pl.ds(pl.multiple_of(t * 128, 128), 128)
    per = [jnp.broadcast_to(table[pl.ds(i, 1), lanes], (16, 128)) for i in range(8)]
    for s in range(8):
        total = per[0] * coef[s, 0:16, lanes].astype(F32)
        for i in range(1, 8):
            total += per[i] * coef[s, i * 16 : i * 16 + 16, lanes].astype(F32)
        turned[pl.ds(s, 16, stride=8), :] = total
    parts = [turned[i * 32 : i * 32 + 32, :] for i in range(4)]
    return swap_blocks(parts, 32)


def output_group(rb, out, x):
    for pair in range(2):
        parts = [rb[x * 16 + b, pair * 16 : pair * 16 + 16, :].astype(F32) for b in range(16)]
        for k in range(2):
            block = jnp.concatenate([p[k * 8 : k * 8 + 8] for p in parts], axis=0).T
            for i in range(4):
                out[x * 16 + i * 4 + pair * 2 + k] = block[i * 32 : i * 32 + 32]


def kernel(
    modes_hbm, order_hbm, widths_hbm, sky_hbm, leg_hbm, out_ref,
    modes, order, widths, xbuf, tab_a, tab_b, table, rows, sb1, rb1, perm, left, turned2, leg,
    coef, even, odd, sums, per_ell, onehot, factors, part, got, matrix, spread, turned, sb3, rb3,
    small_sem, sky_sem, leg_sem, send1, recv1, fsend, frecv, send2, recv2, send3, recv3, own,
):
    me = Place()
    x, c, b = me.x, me.c, me.b
    small = [
        pltpu.make_async_copy(modes_hbm, modes, small_sem.at[0]),
        pltpu.make_async_copy(order_hbm, order, small_sem.at[1]),
        pltpu.make_async_copy(widths_hbm, widths, small_sem.at[2]),
    ]
    for copy in small:
        copy.start()
    for n in range(CHUNKS):
        sky_copy(sky_hbm, xbuf, sky_sem, n).start()
    barrier = pltpu.get_barrier_semaphore()
    for i in range(4):
        for dy, dz in OFFSETS:
            if i or dy or dz:
                device = me.device(wrap(x + i), wrap(me.y + dy), wrap(me.z + dz))
                pl.semaphore_signal(barrier, device_id=device, device_id_type=MESH)
    for device in sum(me.along(1 - c), [me.partner]):
        pl.semaphore_signal(barrier, device_id=device, device_id_type=MESH)
    for copy in small:
        copy.wait()
    make_tables(modes, tab_a, tab_b)
    fourier_rows(sky_hbm, xbuf, sky_sem, tab_a, tab_b, table, rows)
    for u in range(8):
        legendre_copy(leg_hbm, leg, leg_sem, c, u).start()
    pl.semaphore_wait(barrier, 73)

    def swapped(i):
        xx = wrap(x + i)
        parts = [
            rows[half, pl.ds(xx * 8 + k, 16, stride=32), :].astype(BF16) for k in range(8) for half in range(2)
        ]
        return swap_blocks(parts, 8)

    def send_group(i):
        xx = wrap(x + i)
        for dy, dz in OFFSETS:
            if i or dy or dz:
                yy, zz = wrap(me.y + dy), wrap(me.z + dz)
                remote(
                    sb1.at[xx * 16 + yy * 4 + zz], rb1.at[c, me.p], send1, recv1.at[x],
                    me.device(xx, yy, zz),
                ).start()

    last = None
    for i in (2, 1, 3, 0):
        blocks = swapped(i)
        if last is not None:
            send_group(last)
        for g, block in enumerate(blocks):
            sb1[wrap(x + i) * 16 + g] = block
        last = i
    send_group(0)
    local = pltpu.make_async_copy(sb1.at[me.p], rb1.at[c, me.p], own)
    local.start()
    bin_columns(widths, c, onehot)
    mode_factors(modes, b, factors)
    q = lax.broadcasted_iota(jnp.int32, (256, 256), 0)
    perm[...] = jnp.where(q == order[...], 1.0, 0.0).astype(BF16)
    local.wait()

    def forward(core, g):
        lines = pl.ds(g * 16, 16)
        return remote(
            rb1.at[core, lines], rb1.at[core, lines], fsend.at[g], frecv.at[g], me.partner
        )

    for i in (2, 1, 3, 0):
        g = wrap(x + i)
        wait_blocks(rb1.at[c], recv1.at[g], 16 if i else 15)
        forward(c, g).start()
        order_channel(rb1, perm, left, turned2.at[0], c, g)
    for i in (2, 1, 3, 0):
        g = wrap(x + i)
        forward(1 - c, g).wait_recv()
        order_channel(rb1, perm, left, turned2.at[1], 1 - c, g)

    legendre_spectra(
        leg_hbm, leg, leg_sem, c, left, coef, even, odd, factors, sums, per_ell, onehot, part.at[0]
    )
    sum_over_devices(me, part, got, send2, recv2)
    weights = solve_bins(part.at[3], matrix)
    spread[...] = split_dot(weights, onehot[...], NN)

    def tiles(xx, lines):
        made = [
            weighted_tile(coef, spread, turned.at[i], xx * 4 + yy) for i, yy in enumerate(lines)
        ]
        for yy, blocks in zip(lines, made):
            for zz, block in enumerate(blocks):
                sb3[xx * 16 + yy * 4 + zz] = block.astype(BF16)

    def send_tile(xx, yy, places):
        for zz in places:
            remote(
                sb3.at[xx * 16 + yy * 4 + zz], rb3.at[me.p], send3, recv3.at[x],
                me.device(xx, yy, zz),
            ).start()

    def pair(n, _):
        xx = wrap(x + 1 + n // 2)
        lines = [wrap(me.y + 1 + n % 2 * 2), wrap(me.y + 2 + n % 2 * 2)]
        tiles(xx, lines)
        for yy in lines:
            send_tile(xx, yy, range(4))
        return 0

    lax.fori_loop(0, 7, pair, 0)
    lines = [wrap(me.y + 3), me.y]
    tiles(x, lines)
    send_tile(x, lines[0], range(4))
    send_tile(x, me.y, [wrap(me.z + d) for d in (2, 1, 3)])
    local = pltpu.make_async_copy(sb3.at[me.p], rb3.at[me.p], own)
    local.start()
    wait_blocks(got, send2, 13)
    for g in range(4):
        forward(c, g).wait_send()
    wait_blocks(sb1, send1, 63)
    local.wait()
    for i in (3, 2, 1, 0):
        g = wrap(x + i)
        wait_blocks(rb3, recv3.at[g], 16 if i else 15)
        output_group(rb3, out_ref, g)
    wait_blocks(sb3, send3, 63)


def on_device(sky_maps, legendre, mode_values, cycle_order, bin_widths):
    hbm = pl.BlockSpec(memory_space=pltpu.HBM)
    out = pl.pallas_call(
        kernel,
        out_shape=jax.ShapeDtypeStruct((64, 32, 128), F32),
        in_specs=[hbm] * 5,
        out_specs=pl.BlockSpec(memory_space=pltpu.VMEM),
        scratch_shapes=[
            VMEM((1, 128), jnp.int32),
            VMEM((1, 256), jnp.int32),
            VMEM((1, 128), jnp.int32),
            VMEM((CHUNKS, 512, WIDTH), BF16),
            VMEM((2, 64, 128), F32),
            VMEM((2, 128, 128), F32),
            VMEM((2, WIDTH, 256), BF16),
            VMEM((2, 512, 128), F32),
            VMEM((64, 16, 128), BF16),
            VMEM((2, 64, 16, 128), BF16),
            VMEM((256, 256), BF16),
            VMEM((8, 128, 256), BF16),
            VMEM((2, 2, 128, 128), F32),
            VMEM((8, 8, 256, 256), BF16),
            VMEM((8, 128, 2048), BF16),
            VMEM((8, 128, 256), BF16),
            VMEM((8, 128, 256), BF16),
            VMEM((2, 2, PROWS * 8, 128), F32),
            VMEM((2, PROWS, 256), F32),
            VMEM((128, 2048), BF16),
            VMEM((8, 128), F32),
            VMEM((4, PROWS, 128), F32),
            VMEM((21, PROWS, 128), F32),
            VMEM((8, 8, 128), F32),
            VMEM((8, 2048), F32),
            VMEM((2, 128, 128), F32),
            VMEM((64, 32, 128), BF16),
            VMEM((64, 32, 128), BF16),
            DMA((3,)),
            DMA((CHUNKS,)),
            DMA((8,)),
            DMA,
            DMA((4,)),
            DMA((4,)),
            DMA((4,)),
            DMA,
            DMA((9,)),
            DMA,
            DMA((4,)),
            DMA,
        ],
        compiler_params=pltpu.CompilerParams(
            collective_id=0, has_side_effects=True, vmem_limit_bytes=48 << 20
        ),
        name="harmonic_ilc",
    )(
        pltpu.with_memory_space_constraint(mode_values.reshape(1, 128), pltpu.HBM),
        pltpu.with_memory_space_constraint(cycle_order.reshape(1, 256), pltpu.HBM),
        pltpu.with_memory_space_constraint(bin_widths.reshape(1, 128), pltpu.HBM),
        pltpu.with_memory_space_constraint(sky_maps.reshape(512, PIX), pltpu.HBM),
        pltpu.with_memory_space_constraint(legendre, pltpu.HBM),
    )
    return out.reshape(32, 2, 32, 128).transpose(0, 1, 3, 2)


def solution(mesh):
    return jax.shard_map(
        on_device,
        mesh=mesh,
        in_specs=(P("freq", "blk", None, None), P("blk", None, None), P(), P(), P()),
        out_specs=P(None, None, None, ("freq", "blk")),
        check_vma=False,
    )
```

```python
import math

import jax
import jax.numpy as jnp
from jax import lax
from jax.experimental import pallas as pl
from jax.experimental.pallas import tpu as pltpu
from jax.sharding import PartitionSpec as P

F32 = jnp.float32
BF16 = jnp.bfloat16
PIX = 8192
CHUNKS = 4
TURNS = PIX // CHUNKS // 128
WIDTH = PIX // CHUNKS
PAIRS = [(i, j) for i in range(8) for j in range(i, 8)]
PROWS = 40
PARTS = [(0, 16), (16, 16), (32, 8)]
MESH = pl.DeviceIdType.MESH
VMEM = pltpu.VMEM
DMA = pltpu.SemaphoreType.DMA
NN = (((1,), (0,)), ((), ()))
NT = (((1,), (1,)), ((), ()))


def hops(d):
    return min(d, 4 - d)


OFFSETS = sorted(((dy, dz) for dy in range(4) for dz in range(4)), key=lambda t: -hops(t[0]) - hops(t[1]))


def split_dot(a, b, dims):
    count = a.shape[0]
    hi = a.astype(BF16).astype(F32)
    mid = (a - hi).astype(BF16).astype(F32)
    low = a - hi - mid
    parts = jnp.concatenate([low, mid, hi], axis=0).astype(BF16)
    out = lax.dot_general(parts, b, dims, preferred_element_type=F32)
    return out[:count] + out[count : 2 * count] + out[2 * count :]


def swap_blocks(arrays, width):
    count = len(arrays)
    block = lax.broadcasted_iota(jnp.int32, arrays[0].shape, 1) // width
    arrays = list(arrays)
    step = 1
    while step < count:
        low = (block // step) % 2 == 0
        for i in range(count):
            if i & step:
                continue
            a, b = arrays[i], arrays[i | step]
            arrays[i] = jnp.where(low, a, pltpu.roll(b, step * width, 1))
            arrays[i | step] = jnp.where(low, pltpu.roll(a, 128 - step * width, 1), b)
        step *= 2
    return arrays


def turn(phase):
    quadrant = jnp.right_shift(phase + PIX // 8, 11)
    a = (phase - jnp.left_shift(quadrant, 11)).astype(F32) * jnp.float32(2.0 * math.pi / PIX)
    a2 = a * a
    s = jnp.float32(1 / 362880)
    for coefficient in (-1 / 5040, 1 / 120, -1 / 6, 1.0):
        s = s * a2 + jnp.float32(coefficient)
    s = s * a
    c = jnp.float32(-1 / 3628800)
    for coefficient in (1 / 40320, -1 / 720, 1 / 24, -1 / 2, 1.0):
        c = c * a2 + jnp.float32(coefficient)
    odd = (quadrant & 1) == 1
    cosine = jnp.where(odd, s, c)
    sine = jnp.where(odd, c, s)
    cosine = jnp.where(((quadrant + 1) & 2) == 2, -cosine, cosine)
    sine = jnp.where((quadrant & 2) == 2, -sine, sine)
    return cosine, sine


def wrap(v):
    return lax.rem(v, 4)


class Place:
    def __init__(self):
        freq = lax.axis_index("freq")
        self.b = lax.axis_index("blk")
        self.x, self.c = lax.div(freq, 2), lax.rem(freq, 2)
        self.y, self.z = lax.div(self.b, 4), lax.rem(self.b, 4)
        self.p = self.x * 16 + self.b
        self.partner = (self.x * 2 + 1 - self.c, self.b)

    def device(self, x, y, z, core=None):
        return (x * 2 + (self.c if core is None else core), y * 4 + z)

    def along(self, core=None):
        x, y, z = self.x, self.y, self.z
        return [
            [self.device(x, y, wrap(z + d), core) for d in (2, 1, 3)],
            [self.device(x, wrap(y + d), z, core) for d in (2, 1, 3)],
            [self.device(wrap(x + d), y, z, core) for d in (2, 1, 3)],
        ]


def remote(src, dst, send, recv, device):
    return pltpu.make_async_remote_copy(
        src_ref=src, dst_ref=dst, send_sem=send, recv_sem=recv, device_id=device, device_id_type=MESH
    )


def wait_blocks(blocks, sem, count):
    part = blocks.at[pl.ds(0, count)]
    pltpu.make_async_copy(part, part, sem).wait()


def sky_copy(sky_hbm, xbuf, sem, n):
    return pltpu.make_async_copy(
        sky_hbm.at[:, pl.ds(pl.multiple_of(n * WIDTH, WIDTH), WIDTH)], xbuf.at[n], sem.at[n]
    )


def make_tables(modes, tab_a, tab_b):
    m = modes[...]
    factor = jnp.float32(PIX ** (-0.5))
    high = lax.broadcasted_iota(jnp.int32, (64, 128), 0)
    cosine, sine = turn(jnp.left_shift((high * m) & 63, 7))
    tab_a[0] = cosine * factor
    tab_a[1] = sine * factor
    low = lax.broadcasted_iota(jnp.int32, (128, 128), 0)
    cosine, sine = turn((low * m) & (PIX - 1))
    tab_b[0] = cosine
    tab_b[1] = sine


def make_chunk(tab_a, tab_b, table, n):
    for u in range(TURNS):
        ca = tab_a[0, pl.ds(n * TURNS + u, 1), :]
        sa = tab_a[1, pl.ds(n * TURNS + u, 1), :]
        lines = slice(u * 128, u * 128 + 128)
        table[lines, 0:128] = (tab_b[0] * ca - tab_b[1] * sa).astype(BF16)
        table[lines, 128:256] = (tab_b[1] * (-ca) - tab_b[0] * sa).astype(BF16)


def fourier_rows(sky_hbm, xbuf, sem, tab_a, tab_b, table, rows):
    make_chunk(tab_a, tab_b, table.at[0], 0)
    rows[...] = jnp.zeros_like(rows)

    def chunk(n, _):
        sky_copy(sky_hbm, xbuf, sem, n).wait()
        now = lax.rem(n, 2)
        out = jnp.dot(xbuf[n], table[now], preferred_element_type=F32)
        make_chunk(tab_a, tab_b, table.at[1 - now], lax.rem(n + 1, CHUNKS))
        rows[0] += out[:, :128]
        rows[1] += out[:, 128:]
        return 0

    lax.fori_loop(0, CHUNKS, chunk, 0)


def legendre_copy(leg_hbm, leg, sem, c, u):
    start = (u // 2 * 2 + c) * 512 + u % 2 * 256
    return pltpu.make_async_copy(
        leg_hbm.at[:, :, pl.ds(pl.multiple_of(start, 256), 256)], leg.at[u], sem.at[u]
    )


def bin_columns(widths, c, onehot):
    row = lax.broadcasted_iota(jnp.int32, (128, 128), 0)
    col = lax.broadcasted_iota(jnp.int32, (128, 128), 1)
    upper = jnp.where(row <= col, 1.0, 0.0).astype(BF16)
    wide = jnp.broadcast_to(widths[...].astype(F32), (8, 128))
    ends = split_dot(wide, upper, NN)
    begins = ends - wide
    ends = jnp.broadcast_to(ends[0:1], (128, 128)).T
    begins = jnp.broadcast_to(begins[0:1], (128, 128)).T
    lane = lax.broadcasted_iota(jnp.int32, (128, 128), 1)

    def tile(t, _):
        ell = (lane + ((t // 4 * 2 + c) * 512 + t % 4 * 128)).astype(F32)
        hit = jnp.where(ell >= begins, 1.0, 0.0) * jnp.where(ell < ends, 1.0, 0.0)
        onehot[:, pl.ds(pl.multiple_of(t * 128, 128), 128)] = hit.astype(BF16)
        return 0

    lax.fori_loop(0, 16, tile, 0)


def mode_factors(modes, b, factors):
    lane = lax.broadcasted_iota(jnp.int32, (1, 128), 1)
    factor = (1 + jnp.minimum(modes[...], 1)).astype(F32)
    for s in range(8):
        one = jnp.sum(jnp.where(lane == b * 8 + s, factor, 0.0), axis=1, keepdims=True)
        factors[pl.ds(s, 1), :] = jnp.broadcast_to(one, (1, 128))


def order_channel(rb, perm, left, turned, core, g):
    ch = g * 2 + core
    block = rb[core, pl.ds(pl.multiple_of(g * 16, 16), 16)].reshape(256, 128)
    sorted_rows = jnp.dot(perm[...], block, preferred_element_type=F32)
    for h in range(2):
        turned[h] = sorted_rows[h * 128 : h * 128 + 128].T
    for h in range(2):
        for s in range(8):
            left[s, pl.ds(pl.multiple_of(ch * 16, 16), 16), h * 128 : h * 128 + 128] = turned[
                h, pl.ds(s, 16, stride=8), :
            ].astype(BF16)


def legendre_group(leg, left, coef, fresh, u, slots=(0, 8)):
    lanes = pl.ds(pl.multiple_of(u * 256, 256), 256)
    for j in range(slots[1]):
        s = slots[0] + j
        out = jnp.dot(left[s], leg[u, s], preferred_element_type=F32).astype(BF16)
        fresh[s] = out
        coef[s, :, lanes] = out


def spectra_tile(fresh, factors, sums, per_ell, h):
    lanes = pl.ds(pl.multiple_of(h * 128, 128), 128)
    acc = [None] * len(PAIRS)
    for s in range(8):
        both = [fresh[s, i * 16 : i * 16 + 16, lanes].astype(F32) for i in range(8)]
        factor = factors[pl.ds(s, 1), :]
        for half in range(2):
            values = [v[half * 8 : half * 8 + 8] for v in both]
            scaled = [v * factor for v in values]
            for n, (i, j) in enumerate(PAIRS):
                product = scaled[i] * values[j]
                acc[n] = product if acc[n] is None else acc[n] + product
    for n, value in enumerate(acc):
        sums[n * 8 : n * 8 + 8, :] = value
    line = sums[pl.ds(0, PROWS, stride=8), :]
    for r in range(1, 8):
        line = line + sums[pl.ds(r, PROWS, stride=8), :]
    per_ell[:, lanes] = line


def bin_group(per_ell, onehot, total, u):
    group = pl.ds(pl.multiple_of(u * 256, 256), 256)
    total[...] += split_dot(per_ell[...], onehot[:, group], NT)


def legendre_spectra(
    leg_hbm, leg, sem, c, left, coef, even, odd, factors, sums, per_ell, onehot, total
):
    sums[...] = jnp.zeros_like(sums)
    total[...] = jnp.zeros_like(total)
    for u in range(8):
        legendre_copy(leg_hbm, leg, sem, c, u).wait()
    legendre_group(leg, left, coef, even, 0)

    def beside(make, made, u, last=False):
        def half(h, _):
            if not last:
                legendre_group(leg, left, coef, make, u + 1, (h * 4, 4))
            spectra_tile(made, factors, sums.at[0], per_ell.at[0], h)
            return 0

        lax.fori_loop(0, 2, half, 0)
        bin_group(per_ell.at[0], onehot, total, u)

    def step(v, _):
        beside(odd, even, v * 2)
        beside(even, odd, v * 2 + 1)
        return 0

    lax.fori_loop(0, 3, step, 0)
    beside(odd, even, 6)
    beside(even, odd, 7, last=True)


def sum_over_devices(me, part, got, send, recv):
    near, far = me.along(), me.along(1 - me.c)

    def go(stage, index):
        lines = pl.ds(*PARTS[index])
        axis = (stage + index) % 3
        devices = near[axis]
        if stage == 2:
            devices = near[axis] + far[axis] + [me.partner]
        for d, device in enumerate(devices):
            remote(
                part.at[stage, lines], got.at[stage * 7 + d, lines], send,
                recv.at[stage * 3 + index], device,
            ).start()
        return len(devices)

    counts = [go(0, index) for index in range(3)]
    for stage in range(3):
        later = []
        for index in range(3):
            lines = pl.ds(*PARTS[index])
            arrived = got.at[pl.ds(stage * 7, counts[index]), lines]
            pltpu.make_async_copy(arrived, arrived, recv.at[stage * 3 + index]).wait()
            value = part[stage, lines, :]
            for d in range(counts[index]):
                value = value + got[stage * 7 + d, lines, :]
            part[stage + 1, lines, :] = value
            if stage < 2:
                later.append(go(stage + 1, index))
        counts = later


def solve_bins(packed, matrix):
    for row, (i, j) in enumerate(PAIRS):
        value = packed[pl.ds(row, 1), :]
        matrix[j, pl.ds(i, 1), :] = value
        if i != j:
            matrix[i, pl.ds(j, 1), :] = value
    columns = [matrix[j] for j in range(8)]
    rows = lax.broadcasted_iota(jnp.int32, (8, 128), 0)
    trace = sum(columns[j][j : j + 1] for j in range(8))
    load = jnp.float32(0.1) * trace / jnp.float32(8)
    columns = [columns[j] + jnp.where(rows == j, load, 0.0) for j in range(8)]
    z = jnp.ones((8, 128), F32)
    for j in range(8):
        pivot = columns[j][j : j + 1]
        scale = columns[j] / pivot
        keep = rows == j
        for k in range(j + 1, 8):
            columns[k] = columns[k] - jnp.where(keep, 0.0, scale * columns[k][j : j + 1])
        z = z - jnp.where(keep, 0.0, scale * z[j : j + 1])
        columns[j] = jnp.where(keep, columns[j], 0.0)
    z = z / sum(columns)
    return z / jnp.sum(z, axis=0, keepdims=True)


def weighted_tile(coef, table, turned, t):
    lanes = pl.ds(pl.multiple_of(t * 128, 128), 128)
    per = [jnp.broadcast_to(table[pl.ds(i, 1), lanes], (16, 128)) for i in range(8)]
    for s in range(8):
        total = per[0] * coef[s, 0:16, lanes].astype(F32)
        for i in range(1, 8):
            total += per[i] * coef[s, i * 16 : i * 16 + 16, lanes].astype(F32)
        turned[pl.ds(s, 16, stride=8), :] = total
    parts = [turned[i * 32 : i * 32 + 32, :] for i in range(4)]
    return swap_blocks(parts, 32)


def output_group(rb, out, x):
    for pair in range(2):
        parts = [rb[x * 16 + b, pair * 16 : pair * 16 + 16, :].astype(F32) for b in range(16)]
        for k in range(2):
            block = jnp.concatenate([p[k * 8 : k * 8 + 8] for p in parts], axis=0).T
            for i in range(4):
                out[x * 16 + i * 4 + pair * 2 + k] = block[i * 32 : i * 32 + 32]


def kernel(
    modes_hbm, order_hbm, widths_hbm, sky_hbm, leg_hbm, out_ref,
    modes, order, widths, xbuf, tab_a, tab_b, table, rows, sb1, rb1, perm, left, turned2, leg,
    coef, even, odd, sums, per_ell, onehot, factors, part, got, matrix, spread, turned, sb3, rb3,
    small_sem, sky_sem, leg_sem, send1, recv1, fsend, frecv, send2, recv2, send3, recv3, own,
):
    me = Place()
    x, c, b = me.x, me.c, me.b
    small = [
        pltpu.make_async_copy(modes_hbm, modes, small_sem.at[0]),
        pltpu.make_async_copy(order_hbm, order, small_sem.at[1]),
        pltpu.make_async_copy(widths_hbm, widths, small_sem.at[2]),
    ]
    for copy in small:
        copy.start()
    for n in range(CHUNKS):
        sky_copy(sky_hbm, xbuf, sky_sem, n).start()
    barrier = pltpu.get_barrier_semaphore()
    for i in range(4):
        for dy, dz in OFFSETS:
            if i or dy or dz:
                device = me.device(wrap(x + i), wrap(me.y + dy), wrap(me.z + dz))
                pl.semaphore_signal(barrier, device_id=device, device_id_type=MESH)
    for device in sum(me.along(1 - c), [me.partner]):
        pl.semaphore_signal(barrier, device_id=device, device_id_type=MESH)
    for copy in small:
        copy.wait()
    make_tables(modes, tab_a, tab_b)
    fourier_rows(sky_hbm, xbuf, sky_sem, tab_a, tab_b, table, rows)
    for u in range(8):
        legendre_copy(leg_hbm, leg, leg_sem, c, u).start()
    pl.semaphore_wait(barrier, 73)

    def swapped(i):
        xx = wrap(x + i)
        parts = [
            rows[half, pl.ds(xx * 8 + k, 16, stride=32), :].astype(BF16) for k in range(8) for half in range(2)
        ]
        return swap_blocks(parts, 8)

    def send_group(i):
        xx = wrap(x + i)
        for dy, dz in OFFSETS:
            if i or dy or dz:
                yy, zz = wrap(me.y + dy), wrap(me.z + dz)
                remote(
                    sb1.at[xx * 16 + yy * 4 + zz], rb1.at[c, me.p], send1, recv1.at[x],
                    me.device(xx, yy, zz),
                ).start()

    last = None
    for i in (2, 1, 3, 0):
        blocks = swapped(i)
        if last is not None:
            send_group(last)
        for g, block in enumerate(blocks):
            sb1[wrap(x + i) * 16 + g] = block
        last = i
    send_group(0)
    local = pltpu.make_async_copy(sb1.at[me.p], rb1.at[c, me.p], own)
    local.start()
    bin_columns(widths, c, onehot)
    mode_factors(modes, b, factors)
    q = lax.broadcasted_iota(jnp.int32, (256, 256), 0)
    perm[...] = jnp.where(q == order[...], 1.0, 0.0).astype(BF16)
    local.wait()

    def forward(core, g):
        lines = pl.ds(g * 16, 16)
        return remote(
            rb1.at[core, lines], rb1.at[core, lines], fsend.at[g], frecv.at[g], me.partner
        )

    for i in (2, 1, 3, 0):
        g = wrap(x + i)
        wait_blocks(rb1.at[c], recv1.at[g], 16 if i else 15)
        forward(c, g).start()
        order_channel(rb1, perm, left, turned2.at[0], c, g)
    for i in (2, 1, 3, 0):
        g = wrap(x + i)
        forward(1 - c, g).wait_recv()
        order_channel(rb1, perm, left, turned2.at[1], 1 - c, g)

    legendre_spectra(
        leg_hbm, leg, leg_sem, c, left, coef, even, odd, factors, sums, per_ell, onehot, part.at[0]
    )
    sum_over_devices(me, part, got, send2, recv2)
    weights = solve_bins(part.at[3], matrix)
    spread[...] = split_dot(weights, onehot[...], NN)

    def tiles(columns, yy):
        made = [
            weighted_tile(coef, spread, turned.at[i], xx * 4 + yy) for i, xx in enumerate(columns)
        ]
        for xx, blocks in zip(columns, made):
            for zz, block in enumerate(blocks):
                sb3[xx * 16 + yy * 4 + zz] = block.astype(BF16)

    def send_tile(xx, yy, places):
        for zz in places:
            remote(
                sb3.at[xx * 16 + yy * 4 + zz], rb3.at[me.p], send3, recv3.at[x],
                me.device(xx, yy, zz),
            ).start()

    def pair(n, _):
        columns = [wrap(x + 1 + n // 4), wrap(x + 3 + n // 4)]
        yy = wrap(me.y + 1 + n % 4)
        tiles(columns, yy)
        for xx in columns:
            send_tile(xx, yy, range(4))
        return 0

    lax.fori_loop(0, 7, pair, 0)
    columns = [wrap(x + 2), x]
    tiles(columns, me.y)
    send_tile(columns[0], me.y, range(4))
    send_tile(x, me.y, [wrap(me.z + d) for d in (2, 1, 3)])
    local = pltpu.make_async_copy(sb3.at[me.p], rb3.at[me.p], own)
    local.start()
    wait_blocks(got, send2, 13)
    for g in range(4):
        forward(c, g).wait_send()
    wait_blocks(sb1, send1, 63)
    local.wait()
    for i in (3, 1, 2, 0):
        g = wrap(x + i)
        wait_blocks(rb3, recv3.at[g], 16 if i else 15)
        output_group(rb3, out_ref, g)
    wait_blocks(sb3, send3, 63)


def on_device(sky_maps, legendre, mode_values, cycle_order, bin_widths):
    hbm = pl.BlockSpec(memory_space=pltpu.HBM)
    out = pl.pallas_call(
        kernel,
        out_shape=jax.ShapeDtypeStruct((64, 32, 128), F32),
        in_specs=[hbm] * 5,
        out_specs=pl.BlockSpec(memory_space=pltpu.VMEM),
        scratch_shapes=[
            VMEM((1, 128), jnp.int32),
            VMEM((1, 256), jnp.int32),
            VMEM((1, 128), jnp.int32),
            VMEM((CHUNKS, 512, WIDTH), BF16),
            VMEM((2, 64, 128), F32),
            VMEM((2, 128, 128), F32),
            VMEM((2, WIDTH, 256), BF16),
            VMEM((2, 512, 128), F32),
            VMEM((64, 16, 128), BF16),
            VMEM((2, 64, 16, 128), BF16),
            VMEM((256, 256), BF16),
            VMEM((8, 128, 256), BF16),
            VMEM((2, 2, 128, 128), F32),
            VMEM((8, 8, 256, 256), BF16),
            VMEM((8, 128, 2048), BF16),
            VMEM((8, 128, 256), BF16),
            VMEM((8, 128, 256), BF16),
            VMEM((1, PROWS * 8, 128), F32),
            VMEM((1, PROWS, 256), F32),
            VMEM((128, 2048), BF16),
            VMEM((8, 128), F32),
            VMEM((4, PROWS, 128), F32),
            VMEM((21, PROWS, 128), F32),
            VMEM((8, 8, 128), F32),
            VMEM((8, 2048), F32),
            VMEM((2, 128, 128), F32),
            VMEM((64, 32, 128), BF16),
            VMEM((64, 32, 128), BF16),
            DMA((3,)),
            DMA((CHUNKS,)),
            DMA((8,)),
            DMA,
            DMA((4,)),
            DMA((4,)),
            DMA((4,)),
            DMA,
            DMA((9,)),
            DMA,
            DMA((4,)),
            DMA,
        ],
        compiler_params=pltpu.CompilerParams(
            collective_id=0, has_side_effects=True, vmem_limit_bytes=48 << 20
        ),
        name="harmonic_ilc",
    )(
        pltpu.with_memory_space_constraint(mode_values.reshape(1, 128), pltpu.HBM),
        pltpu.with_memory_space_constraint(cycle_order.reshape(1, 256), pltpu.HBM),
        pltpu.with_memory_space_constraint(bin_widths.reshape(1, 128), pltpu.HBM),
        pltpu.with_memory_space_constraint(sky_maps.reshape(512, PIX), pltpu.HBM),
        pltpu.with_memory_space_constraint(legendre, pltpu.HBM),
    )
    return out.reshape(32, 2, 32, 128).transpose(0, 1, 3, 2)


def solution(mesh):
    return jax.shard_map(
        on_device,
        mesh=mesh,
        in_specs=(P("freq", "blk", None, None), P("blk", None, None), P(), P(), P()),
        out_specs=P(None, None, None, ("freq", "blk")),
        check_vma=False,
    )
```

```python
import math

import jax
import jax.numpy as jnp
from jax import lax
from jax.experimental import pallas as pl
from jax.experimental.pallas import tpu as pltpu
from jax.sharding import PartitionSpec as P

F32 = jnp.float32
BF16 = jnp.bfloat16
PIX = 8192
CHUNKS = 4
TURNS = PIX // CHUNKS // 128
WIDTH = PIX // CHUNKS
PAIRS = [(i, j) for i in range(8) for j in range(i, 8)]
PROWS = 40
PARTS = [(0, 16), (16, 24)]
MESH = pl.DeviceIdType.MESH
VMEM = pltpu.VMEM
DMA = pltpu.SemaphoreType.DMA
NN = (((1,), (0,)), ((), ()))
NT = (((1,), (1,)), ((), ()))


def hops(d):
    return min(d, 4 - d)


OFFSETS = sorted(((dy, dz) for dy in range(4) for dz in range(4)), key=lambda t: -hops(t[0]) - hops(t[1]))


def split_dot(a, b, dims):
    count = a.shape[0]
    hi = a.astype(BF16).astype(F32)
    mid = (a - hi).astype(BF16).astype(F32)
    low = a - hi - mid
    parts = jnp.concatenate([low, mid, hi], axis=0).astype(BF16)
    out = lax.dot_general(parts, b, dims, preferred_element_type=F32)
    return out[:count] + out[count : 2 * count] + out[2 * count :]


def swap_blocks(arrays, width):
    count = len(arrays)
    block = lax.broadcasted_iota(jnp.int32, arrays[0].shape, 1) // width
    arrays = list(arrays)
    step = 1
    while step < count:
        low = (block // step) % 2 == 0
        for i in range(count):
            if i & step:
                continue
            a, b = arrays[i], arrays[i | step]
            arrays[i] = jnp.where(low, a, pltpu.roll(b, step * width, 1))
            arrays[i | step] = jnp.where(low, pltpu.roll(a, 128 - step * width, 1), b)
        step *= 2
    return arrays


def turn(phase):
    quadrant = jnp.right_shift(phase + PIX // 8, 11)
    a = (phase - jnp.left_shift(quadrant, 11)).astype(F32) * jnp.float32(2.0 * math.pi / PIX)
    a2 = a * a
    s = jnp.float32(1 / 362880)
    for coefficient in (-1 / 5040, 1 / 120, -1 / 6, 1.0):
        s = s * a2 + jnp.float32(coefficient)
    s = s * a
    c = jnp.float32(-1 / 3628800)
    for coefficient in (1 / 40320, -1 / 720, 1 / 24, -1 / 2, 1.0):
        c = c * a2 + jnp.float32(coefficient)
    odd = (quadrant & 1) == 1
    cosine = jnp.where(odd, s, c)
    sine = jnp.where(odd, c, s)
    cosine = jnp.where(((quadrant + 1) & 2) == 2, -cosine, cosine)
    sine = jnp.where((quadrant & 2) == 2, -sine, sine)
    return cosine, sine


def wrap(v):
    return lax.rem(v, 4)


class Place:
    def __init__(self):
        freq = lax.axis_index("freq")
        self.b = lax.axis_index("blk")
        self.x, self.c = lax.div(freq, 2), lax.rem(freq, 2)
        self.y, self.z = lax.div(self.b, 4), lax.rem(self.b, 4)
        self.p = self.x * 16 + self.b
        self.partner = (self.x * 2 + 1 - self.c, self.b)

    def device(self, x, y, z, core=None):
        return (x * 2 + (self.c if core is None else core), y * 4 + z)

    def along(self, core=None):
        x, y, z = self.x, self.y, self.z
        return [
            [self.device(x, y, wrap(z + d), core) for d in (2, 1, 3)],
            [self.device(x, wrap(y + d), z, core) for d in (2, 1, 3)],
            [self.device(wrap(x + d), y, z, core) for d in (2, 1, 3)],
        ]


def remote(src, dst, send, recv, device):
    return pltpu.make_async_remote_copy(
        src_ref=src, dst_ref=dst, send_sem=send, recv_sem=recv, device_id=device, device_id_type=MESH
    )


def wait_blocks(blocks, sem, count):
    part = blocks.at[pl.ds(0, count)]
    pltpu.make_async_copy(part, part, sem).wait()


def sky_copy(sky_hbm, xbuf, sem, n):
    return pltpu.make_async_copy(
        sky_hbm.at[:, pl.ds(pl.multiple_of(n * WIDTH, WIDTH), WIDTH)], xbuf.at[n], sem.at[n]
    )


def make_tables(modes, tab_a, tab_b):
    m = modes[...]
    factor = jnp.float32(PIX ** (-0.5))
    high = lax.broadcasted_iota(jnp.int32, (64, 128), 0)
    cosine, sine = turn(jnp.left_shift((high * m) & 63, 7))
    tab_a[0] = cosine * factor
    tab_a[1] = sine * factor
    low = lax.broadcasted_iota(jnp.int32, (128, 128), 0)
    cosine, sine = turn((low * m) & (PIX - 1))
    tab_b[0] = cosine
    tab_b[1] = sine


def make_chunk(tab_a, tab_b, table, n):
    for u in range(TURNS):
        ca = tab_a[0, pl.ds(n * TURNS + u, 1), :]
        sa = tab_a[1, pl.ds(n * TURNS + u, 1), :]
        lines = slice(u * 128, u * 128 + 128)
        table[lines, 0:128] = (tab_b[0] * ca - tab_b[1] * sa).astype(BF16)
        table[lines, 128:256] = (tab_b[1] * (-ca) - tab_b[0] * sa).astype(BF16)


def fourier_rows(sky_hbm, xbuf, sem, tab_a, tab_b, table, rows):
    make_chunk(tab_a, tab_b, table.at[0], 0)
    rows[...] = jnp.zeros_like(rows)

    def chunk(n, _):
        sky_copy(sky_hbm, xbuf, sem, n).wait()
        now = lax.rem(n, 2)
        out = jnp.dot(xbuf[n], table[now], preferred_element_type=F32)
        make_chunk(tab_a, tab_b, table.at[1 - now], lax.rem(n + 1, CHUNKS))
        rows[0] += out[:, :128]
        rows[1] += out[:, 128:]
        return 0

    lax.fori_loop(0, CHUNKS, chunk, 0)


def legendre_copy(leg_hbm, leg, sem, c, u):
    start = (u // 2 * 2 + c) * 512 + u % 2 * 256
    return pltpu.make_async_copy(
        leg_hbm.at[:, :, pl.ds(pl.multiple_of(start, 256), 256)], leg.at[u], sem.at[u]
    )


def bin_columns(widths, c, onehot):
    row = lax.broadcasted_iota(jnp.int32, (128, 128), 0)
    col = lax.broadcasted_iota(jnp.int32, (128, 128), 1)
    upper = jnp.where(row <= col, 1.0, 0.0).astype(BF16)
    wide = jnp.broadcast_to(widths[...].astype(F32), (8, 128))
    ends = split_dot(wide, upper, NN)
    begins = ends - wide
    ends = jnp.broadcast_to(ends[0:1], (128, 128)).T
    begins = jnp.broadcast_to(begins[0:1], (128, 128)).T
    lane = lax.broadcasted_iota(jnp.int32, (128, 128), 1)

    def tile(t, _):
        ell = (lane + ((t // 4 * 2 + c) * 512 + t % 4 * 128)).astype(F32)
        hit = jnp.where(ell >= begins, 1.0, 0.0) * jnp.where(ell < ends, 1.0, 0.0)
        onehot[:, pl.ds(pl.multiple_of(t * 128, 128), 128)] = hit.astype(BF16)
        return 0

    lax.fori_loop(0, 16, tile, 0)


def mode_factors(modes, b, factors):
    lane = lax.broadcasted_iota(jnp.int32, (1, 128), 1)
    factor = (1 + jnp.minimum(modes[...], 1)).astype(F32)
    for s in range(8):
        one = jnp.sum(jnp.where(lane == b * 8 + s, factor, 0.0), axis=1, keepdims=True)
        factors[pl.ds(s, 1), :] = jnp.broadcast_to(one, (1, 128))


def order_channel(rb, perm, left, turned, core, g):
    ch = g * 2 + core
    block = rb[core, pl.ds(pl.multiple_of(g * 16, 16), 16)].reshape(256, 128)
    sorted_rows = jnp.dot(perm[...], block, preferred_element_type=F32)
    for h in range(2):
        turned[h] = sorted_rows[h * 128 : h * 128 + 128].T
    for h in range(2):
        for s in range(8):
            left[s, pl.ds(pl.multiple_of(ch * 16, 16), 16), h * 128 : h * 128 + 128] = turned[
                h, pl.ds(s, 16, stride=8), :
            ].astype(BF16)


def legendre_group(leg, left, coef, fresh, u, slots=(0, 8)):
    lanes = pl.ds(pl.multiple_of(u * 256, 256), 256)
    for j in range(slots[1]):
        s = slots[0] + j
        out = jnp.dot(left[s], leg[u, s], preferred_element_type=F32).astype(BF16)
        fresh[s] = out
        coef[s, :, lanes] = out


def spectra_tile(fresh, factors, sums, per_ell, h):
    lanes = pl.ds(pl.multiple_of(h * 128, 128), 128)
    acc = [None] * len(PAIRS)
    for s in range(8):
        both = [fresh[s, i * 16 : i * 16 + 16, lanes].astype(F32) for i in range(8)]
        factor = factors[pl.ds(s, 1), :]
        for half in range(2):
            values = [v[half * 8 : half * 8 + 8] for v in both]
            scaled = [v * factor for v in values]
            for n, (i, j) in enumerate(PAIRS):
                product = scaled[i] * values[j]
                acc[n] = product if acc[n] is None else acc[n] + product
    for n, value in enumerate(acc):
        sums[n * 8 : n * 8 + 8, :] = value
    line = sums[pl.ds(0, PROWS, stride=8), :]
    for r in range(1, 8):
        line = line + sums[pl.ds(r, PROWS, stride=8), :]
    per_ell[:, lanes] = line


def bin_group(per_ell, onehot, total, u):
    group = pl.ds(pl.multiple_of(u * 256, 256), 256)
    total[...] += split_dot(per_ell[...], onehot[:, group], NT)


def legendre_spectra(
    leg_hbm, leg, sem, c, left, coef, even, odd, factors, sums, per_ell, onehot, total
):
    sums[...] = jnp.zeros_like(sums)
    total[...] = jnp.zeros_like(total)
    for u in range(8):
        legendre_copy(leg_hbm, leg, sem, c, u).wait()
    legendre_group(leg, left, coef, even, 0)

    def beside(make, made, u, last=False):
        def half(h, _):
            if not last:
                legendre_group(leg, left, coef, make, u + 1, (h * 4, 4))
            spectra_tile(made, factors, sums.at[0], per_ell.at[0], h)
            return 0

        lax.fori_loop(0, 2, half, 0)
        bin_group(per_ell.at[0], onehot, total, u)

    def step(v, _):
        beside(odd, even, v * 2)
        beside(even, odd, v * 2 + 1)
        return 0

    lax.fori_loop(0, 3, step, 0)
    beside(odd, even, 6)
    beside(even, odd, 7, last=True)


def sum_over_devices(me, part, got, send, recv):
    near, far = me.along(), me.along(1 - me.c)
    groups = [
        [me.device(me.x, wrap(me.y + dy), wrap(me.z + dz)) for dy, dz in OFFSETS if dy or dz],
        near[2] + far[2] + [me.partner],
    ]

    def go(stage, index):
        lines = pl.ds(*PARTS[index])
        devices = groups[(stage + index) % 2]
        for d, device in enumerate(devices):
            remote(
                part.at[stage, lines], got.at[stage * 15 + d, lines], send,
                recv.at[stage * 2 + index], device,
            ).start()
        return len(devices)

    counts = [go(0, index) for index in range(2)]
    for stage in range(2):
        later = []
        for index in range(2):
            lines = pl.ds(*PARTS[index])
            arrived = got.at[pl.ds(stage * 15, counts[index]), lines]
            pltpu.make_async_copy(arrived, arrived, recv.at[stage * 2 + index]).wait()
            value = part[stage, lines, :]
            for d in range(counts[index]):
                value = value + got[stage * 15 + d, lines, :]
            part[stage + 1, lines, :] = value
            if stage < 1:
                later.append(go(stage + 1, index))
        counts = later


def solve_bins(packed, matrix):
    for row, (i, j) in enumerate(PAIRS):
        value = packed[pl.ds(row, 1), :]
        matrix[j, pl.ds(i, 1), :] = value
        if i != j:
            matrix[i, pl.ds(j, 1), :] = value
    columns = [matrix[j] for j in range(8)]
    rows = lax.broadcasted_iota(jnp.int32, (8, 128), 0)
    trace = sum(columns[j][j : j + 1] for j in range(8))
    load = jnp.float32(0.1) * trace / jnp.float32(8)
    columns = [columns[j] + jnp.where(rows == j, load, 0.0) for j in range(8)]
    z = jnp.ones((8, 128), F32)
    for j in range(8):
        pivot = columns[j][j : j + 1]
        scale = columns[j] / pivot
        keep = rows == j
        for k in range(j + 1, 8):
            columns[k] = columns[k] - jnp.where(keep, 0.0, scale * columns[k][j : j + 1])
        z = z - jnp.where(keep, 0.0, scale * z[j : j + 1])
        columns[j] = jnp.where(keep, columns[j], 0.0)
    z = z / sum(columns)
    return z / jnp.sum(z, axis=0, keepdims=True)


def weighted_tile(coef, table, turned, t):
    lanes = pl.ds(pl.multiple_of(t * 128, 128), 128)
    per = [jnp.broadcast_to(table[pl.ds(i, 1), lanes], (16, 128)) for i in range(8)]
    for s in range(8):
        total = per[0] * coef[s, 0:16, lanes].astype(F32)
        for i in range(1, 8):
            total += per[i] * coef[s, i * 16 : i * 16 + 16, lanes].astype(F32)
        turned[pl.ds(s, 16, stride=8), :] = total
    parts = [turned[i * 32 : i * 32 + 32, :] for i in range(4)]
    return swap_blocks(parts, 32)


def output_group(rb, out, x):
    for pair in range(2):
        parts = [rb[x * 16 + b, pair * 16 : pair * 16 + 16, :].astype(F32) for b in range(16)]
        for k in range(2):
            block = jnp.concatenate([p[k * 8 : k * 8 + 8] for p in parts], axis=0).T
            for i in range(4):
                out[x * 16 + i * 4 + pair * 2 + k] = block[i * 32 : i * 32 + 32]


def kernel(
    modes_hbm, order_hbm, widths_hbm, sky_hbm, leg_hbm, out_ref,
    modes, order, widths, xbuf, tab_a, tab_b, table, rows, sb1, rb1, perm, left, turned2, leg,
    coef, even, odd, sums, per_ell, onehot, factors, part, got, matrix, spread, turned, sb3, rb3,
    small_sem, sky_sem, leg_sem, send1, recv1, fsend, frecv, send2, recv2, send3, recv3, own,
):
    me = Place()
    x, c, b = me.x, me.c, me.b
    small = [
        pltpu.make_async_copy(modes_hbm, modes, small_sem.at[0]),
        pltpu.make_async_copy(order_hbm, order, small_sem.at[1]),
        pltpu.make_async_copy(widths_hbm, widths, small_sem.at[2]),
    ]
    for copy in small:
        copy.start()
    for n in range(CHUNKS):
        sky_copy(sky_hbm, xbuf, sky_sem, n).start()
    barrier = pltpu.get_barrier_semaphore()
    for i in range(4):
        for dy, dz in OFFSETS:
            if i or dy or dz:
                device = me.device(wrap(x + i), wrap(me.y + dy), wrap(me.z + dz))
                pl.semaphore_signal(barrier, device_id=device, device_id_type=MESH)
    for device in sum(me.along(1 - c), [me.partner]):
        pl.semaphore_signal(barrier, device_id=device, device_id_type=MESH)
    for copy in small:
        copy.wait()
    make_tables(modes, tab_a, tab_b)
    fourier_rows(sky_hbm, xbuf, sky_sem, tab_a, tab_b, table, rows)
    for u in range(8):
        legendre_copy(leg_hbm, leg, leg_sem, c, u).start()
    pl.semaphore_wait(barrier, 73)

    def swapped(i):
        xx = wrap(x + i)
        parts = [
            rows[half, pl.ds(xx * 8 + k, 16, stride=32), :].astype(BF16) for k in range(8) for half in range(2)
        ]
        return swap_blocks(parts, 8)

    def send_group(i):
        xx = wrap(x + i)
        for dy, dz in OFFSETS:
            if i or dy or dz:
                yy, zz = wrap(me.y + dy), wrap(me.z + dz)
                remote(
                    sb1.at[xx * 16 + yy * 4 + zz], rb1.at[c, me.p], send1, recv1.at[x],
                    me.device(xx, yy, zz),
                ).start()

    last = None
    for i in (2, 1, 3, 0):
        blocks = swapped(i)
        if last is not None:
            send_group(last)
        for g, block in enumerate(blocks):
            sb1[wrap(x + i) * 16 + g] = block
        last = i
    send_group(0)
    local = pltpu.make_async_copy(sb1.at[me.p], rb1.at[c, me.p], own)
    local.start()
    bin_columns(widths, c, onehot)
    mode_factors(modes, b, factors)
    q = lax.broadcasted_iota(jnp.int32, (256, 256), 0)
    perm[...] = jnp.where(q == order[...], 1.0, 0.0).astype(BF16)
    local.wait()

    def forward(core, g):
        lines = pl.ds(g * 16, 16)
        return remote(
            rb1.at[core, lines], rb1.at[core, lines], fsend.at[g], frecv.at[g], me.partner
        )

    for i in (2, 1, 3, 0):
        g = wrap(x + i)
        wait_blocks(rb1.at[c], recv1.at[g], 16 if i else 15)
        forward(c, g).start()
    for i in (2, 1, 3, 0):
        order_channel(rb1, perm, left, turned2.at[0], c, wrap(x + i))
    for i in (2, 1, 3, 0):
        g = wrap(x + i)
        forward(1 - c, g).wait_recv()
        order_channel(rb1, perm, left, turned2.at[1], 1 - c, g)

    legendre_spectra(
        leg_hbm, leg, leg_sem, c, left, coef, even, odd, factors, sums, per_ell, onehot, part.at[0]
    )
    sum_over_devices(me, part, got, send2, recv2)
    weights = solve_bins(part.at[2], matrix)
    spread[...] = split_dot(weights, onehot[...], NN)

    def tiles(columns, yy):
        made = [
            weighted_tile(coef, spread, turned.at[i], xx * 4 + yy) for i, xx in enumerate(columns)
        ]
        for xx, blocks in zip(columns, made):
            for zz, block in enumerate(blocks):
                sb3[xx * 16 + yy * 4 + zz] = block.astype(BF16)

    def send_tile(xx, yy, places):
        for zz in places:
            remote(
                sb3.at[xx * 16 + yy * 4 + zz], rb3.at[me.p], send3, recv3.at[x],
                me.device(xx, yy, zz),
            ).start()

    def pair(n, _):
        columns = [wrap(x + 1 + n // 4), wrap(x + 3 + n // 4)]
        yy = wrap(me.y + 1 + n % 4)
        tiles(columns, yy)
        for xx in columns:
            send_tile(xx, yy, range(4))
        return 0

    lax.fori_loop(0, 7, pair, 0)
    columns = [wrap(x + 2), x]
    tiles(columns, me.y)
    send_tile(columns[0], me.y, range(4))
    send_tile(x, me.y, [wrap(me.z + d) for d in (2, 1, 3)])
    local = pltpu.make_async_copy(sb3.at[me.p], rb3.at[me.p], own)
    local.start()
    wait_blocks(got, send2, 22)
    for g in range(4):
        forward(c, g).wait_send()
    wait_blocks(sb1, send1, 63)
    local.wait()
    for i in (3, 1, 2, 0):
        g = wrap(x + i)
        wait_blocks(rb3, recv3.at[g], 16 if i else 15)
        output_group(rb3, out_ref, g)
    wait_blocks(sb3, send3, 63)


def on_device(sky_maps, legendre, mode_values, cycle_order, bin_widths):
    hbm = pl.BlockSpec(memory_space=pltpu.HBM)
    out = pl.pallas_call(
        kernel,
        out_shape=jax.ShapeDtypeStruct((64, 32, 128), F32),
        in_specs=[hbm] * 5,
        out_specs=pl.BlockSpec(memory_space=pltpu.VMEM),
        scratch_shapes=[
            VMEM((1, 128), jnp.int32),
            VMEM((1, 256), jnp.int32),
            VMEM((1, 128), jnp.int32),
            VMEM((CHUNKS, 512, WIDTH), BF16),
            VMEM((2, 64, 128), F32),
            VMEM((2, 128, 128), F32),
            VMEM((2, WIDTH, 256), BF16),
            VMEM((2, 512, 128), F32),
            VMEM((64, 16, 128), BF16),
            VMEM((2, 64, 16, 128), BF16),
            VMEM((256, 256), BF16),
            VMEM((8, 128, 256), BF16),
            VMEM((2, 2, 128, 128), F32),
            VMEM((8, 8, 256, 256), BF16),
            VMEM((8, 128, 2048), BF16),
            VMEM((8, 128, 256), BF16),
            VMEM((8, 128, 256), BF16),
            VMEM((1, PROWS * 8, 128), F32),
            VMEM((1, PROWS, 256), F32),
            VMEM((128, 2048), BF16),
            VMEM((8, 128), F32),
            VMEM((4, PROWS, 128), F32),
            VMEM((30, PROWS, 128), F32),
            VMEM((8, 8, 128), F32),
            VMEM((8, 2048), F32),
            VMEM((2, 128, 128), F32),
            VMEM((64, 32, 128), BF16),
            VMEM((64, 32, 128), BF16),
            DMA((3,)),
            DMA((CHUNKS,)),
            DMA((8,)),
            DMA,
            DMA((4,)),
            DMA((4,)),
            DMA((4,)),
            DMA,
            DMA((9,)),
            DMA,
            DMA((4,)),
            DMA,
        ],
        compiler_params=pltpu.CompilerParams(
            collective_id=0, has_side_effects=True, vmem_limit_bytes=48 << 20
        ),
        name="harmonic_ilc",
    )(
        pltpu.with_memory_space_constraint(mode_values.reshape(1, 128), pltpu.HBM),
        pltpu.with_memory_space_constraint(cycle_order.reshape(1, 256), pltpu.HBM),
        pltpu.with_memory_space_constraint(bin_widths.reshape(1, 128), pltpu.HBM),
        pltpu.with_memory_space_constraint(sky_maps.reshape(512, PIX), pltpu.HBM),
        pltpu.with_memory_space_constraint(legendre, pltpu.HBM),
    )
    return out.reshape(32, 2, 32, 128).transpose(0, 1, 3, 2)


def solution(mesh):
    return jax.shard_map(
        on_device,
        mesh=mesh,
        in_specs=(P("freq", "blk", None, None), P("blk", None, None), P(), P(), P()),
        out_specs=P(None, None, None, ("freq", "blk")),
        check_vma=False,
    )
```
